256 devices in a mesh: row: 32 (over x, y, core), col: 8 (over z).
Axes of the slice: x: 4, y: 4, z: 8, core: 2. Of those that a mesh axis runs over, the one named last changes fastest.
Arguments:
- activations: float32 [32768, 8192], P('row', 'col'), may hold values from -120 to 120
- plan: int32 [2, 32], replicated, may hold values from 0 to 31, as said below
Outputs:
- rotated: float32 [32768, 8192], P('row', 'col')
The draws below stay inside these ranges and needn't reach their ends.
Inputs may be any that keep to these rules, and one draw needn't show every extreme that they name: `plan`: row r gives, for every slot, which block of layout 0 stands there in round r; row 0 is the identity and each row is a permutation. Going from one round to the next, all blocks but the one in a fixed slot move one place along the circle of slots formed by the leads in rising order followed by the mates in falling order (the fixed slot is skipped), all in the same sense, so each index of col sends at most one block to each neighbouring index and none farther.
All inputs are finite; a program needn't handle non-finite values.
Results may differ from the reference program's by a relative error of at most 0.0003.
Values sent between devices are 32-bit elements; how exact they have to be, the bound alone decides.
A program may use at most 128 MiB of HBM per device.

```python
import math
import jax
import jax.numpy as jnp
from jax import lax

BLK = 256
ROUNDS = 2
NBLK = 32
NCOL = 8192
ROWS = 32768


def draw_activations(key, part):
    subkeys = jax.random.split(key, 4)
    jitter = jnp.clip(jax.random.normal(subkeys[0], (ROWS, NCOL), jnp.float32), -5.0, 5.0)
    strength = 0.6
    scales = jnp.exp(jax.random.uniform(subkeys[1], (NCOL,), jnp.float32, math.log(0.3), math.log(3.0)))
    shared = jnp.clip(jax.random.normal(subkeys[2], (ROWS,), jnp.float32), -4.0, 4.0)
    loading = jnp.clip(jax.random.normal(subkeys[3], (NCOL,), jnp.float32), -4.0, 4.0)
    row_ramp = 0.6 + 1.2 * jnp.arange(ROWS, dtype=jnp.float32) / (ROWS - 1)
    return row_ramp[:, None] * scales[None, :] * (jitter + strength * shared[:, None] * loading[None, :])


def draw_plan(key, part):
    subkeys = jax.random.split(key, 2)
    firsts = jnp.arange(0, NBLK, 2, dtype=jnp.int32)
    seconds = jnp.arange(NBLK - 1, 0, -2, dtype=jnp.int32)
    circle = jnp.concatenate([firsts, seconds])
    anchor = jax.random.randint(subkeys[0], (), 0, NBLK)
    heading = 2 * jax.random.randint(subkeys[1], (), 0, 2) - 1
    positions = jnp.arange(NBLK - 1, dtype=jnp.int32)
    moving = circle[positions + (positions >= anchor).astype(jnp.int32)]
    rows_out = []
    for round_index in range(ROUNDS):
        shifted = moving[(positions + heading * round_index) % (NBLK - 1)]
        layout = jnp.arange(NBLK, dtype=jnp.int32).at[moving].set(shifted)
        rows_out.append(layout)
    return jnp.stack(rows_out).astype(jnp.int32)


def setup_inputs(seed: int = 0) -> dict:
    keys = jax.random.split(jax.random.key(seed), 3)
    return {
        "activations": draw_activations(jax.random.fold_in(keys[2], 71), 0),
        "plan": draw_plan(jax.random.fold_in(keys[2], 71), 0),
    }


highest = lax.Precision.HIGHEST
epsilon = 1e-06

def inverse_spd(matrix):
    factor = jnp.linalg.cholesky(matrix)
    unit_batch = jnp.broadcast_to(jnp.eye(matrix.shape[-1], dtype=matrix.dtype), matrix.shape)
    inverse_factor = jax.scipy.linalg.solve_triangular(factor, unit_batch, lower=True)
    return jnp.einsum('pba,pbc->pac', inverse_factor, inverse_factor, precision=highest)

def cayley_update(lead_block, mate_block, cross_gram, lead_sq, mate_sq):
    coupling = cross_gram / (lead_sq[:, :, None] + mate_sq[:, None, :] + epsilon)
    identity = jnp.eye(coupling.shape[-1], dtype=jnp.float32)[None, :, :]
    left_gram = identity + 0.25 * jnp.einsum('pab,pcb->pac', coupling, coupling, precision=highest)
    right_gram = identity + 0.25 * jnp.einsum('pba,pbc->pac', coupling, coupling, precision=highest)
    left_inv = inverse_spd(left_gram)
    right_inv = inverse_spd(right_gram)
    mixed_lead = 2.0 * lead_block - jnp.einsum('rpb,pab->rpa', mate_block, coupling, precision=highest)
    mixed_mate = jnp.einsum('rpa,pab->rpb', lead_block, coupling, precision=highest) + 2.0 * mate_block
    new_lead = jnp.einsum('rpa,pab->rpb', mixed_lead, left_inv, precision=highest) - lead_block
    new_mate = jnp.einsum('rpa,pab->rpb', mixed_mate, right_inv, precision=highest) - mate_block
    return (new_lead, new_mate)

def source_slots(earlier_layout, later_layout):
    slot_total = earlier_layout.shape[0]
    matches = later_layout[:, None] == earlier_layout[None, :]
    positions = jnp.arange(slot_total, dtype=jnp.int32)
    return jnp.sum(jnp.where(matches, positions[None, :], 0), axis=1).astype(jnp.int32)

def reference(activations, plan):
    row_count = activations.shape[0]
    slot_total = activations.shape[1] // BLK
    current = activations
    for round_index in range(ROUNDS):
        blocks = current.reshape(row_count, slot_total // 2, 2, BLK)
        lead_block = blocks[:, :, 0, :]
        mate_block = blocks[:, :, 1, :]
        cross_gram = jnp.einsum('rpa,rpb->pab', lead_block, mate_block, precision=highest)
        lead_sq = jnp.sum(lead_block * lead_block, axis=0)
        mate_sq = jnp.sum(mate_block * mate_block, axis=0)
        new_lead, new_mate = cayley_update(lead_block, mate_block, cross_gram, lead_sq, mate_sq)
        current = jnp.stack([new_lead, new_mate], axis=2).reshape(row_count, slot_total * BLK)
        if round_index + 1 < ROUNDS:
            source = source_slots(plan[round_index], plan[round_index + 1])
            current = current.reshape(row_count, slot_total, BLK)[:, source, :].reshape(row_count, slot_total * BLK)
    return current
```

```python
import functools

import jax
import jax.numpy as jnp
from jax import lax
from jax.experimental import pallas as pl
from jax.experimental.pallas import tpu as pltpu
from jax.sharding import PartitionSpec as P

BLK = 256
HALF = 128
EPS = 1e-6
STEPS = 9
BOUND = 1.02 * (1.0 + (BLK / 2) ** 2 / 4)
MESH = pl.DeviceIdType.MESH
HIGHEST = lax.Precision.HIGHEST
f32, bf16 = jnp.float32, jnp.bfloat16


def split(value):
    hi = value.astype(bf16)
    return hi, (value - hi.astype(f32)).astype(bf16)


def mm(a, b):
    return lax.dot_general(a, b, (((1,), (0,)), ((), ())), preferred_element_type=f32)


def mm_t(a, b):
    return lax.dot_general(a, b, (((0,), (0,)), ((), ())), preferred_element_type=f32)


def mm3(a, b):
    return mm(a[0], b[0]) + (mm(a[0], b[1]) + mm(a[1], b[0]))


def full(a, b, dims):
    return lax.dot_general(a, b, (dims, ((), ())), precision=HIGHEST, preferred_element_type=f32)


def eye():
    rows = lax.broadcasted_iota(jnp.int32, (BLK, BLK), 0)
    cols = lax.broadcasted_iota(jnp.int32, (BLK, BLK), 1)
    return jnp.where(rows == cols, 1.0, 0.0).astype(f32)


def put_rotation(q, hi_ref, lo_ref, pair):
    q11, w, q22 = q
    for value, r, c in ((q11, 0, 0), (w, 0, 1), (-w.T, 1, 0), (q22, 1, 1)):
        hi, lo = split(value)
        hi_ref[pair, r * BLK : (r + 1) * BLK, c * BLK : (c + 1) * BLK] = hi
        lo_ref[pair, r * BLK : (r + 1) * BLK, c * BLK : (c + 1) * BLK] = lo


def rounds_kernel(
    n_row, n_col, rows, step_rows,
    plan_ref, x_ref, x2_ref, q_ref,
    xv, nv, zsend, zrecv, gram, sq, part_send, part_recv, rs_src, rs_recv, ag, rx, gmat, cmat, qv, qhi, qlo,
    load_sem, part_s, part_r, rs_s, rs_r, ag_s, ag_r, q_s, q_r, z_s, z_r, out_sem,
):
    chips = n_row // 2
    crow = BLK // chips
    row, z = lax.axis_index("row"), lax.axis_index("col")
    core, chip = lax.rem(row, 2), row // 2
    other = 1 - core
    partner = (chip * 2 + other, z)
    z_up, z_down = lax.rem(z + 1, n_col), lax.rem(z + n_col - 1, n_col)
    n_steps = rows // step_rows

    def peer(k):
        t = lax.rem(chip + k, chips)
        return t, (t * 2 + core, z)

    loads = []
    for i, p in enumerate((other, core)):
        for h in range(2):
            cols = pl.ds(pl.multiple_of((2 * p + h) * BLK, BLK), BLK)
            loads.append(pltpu.make_async_copy(x_ref.at[:, cols], xv.at[2 * p + h], load_sem.at[2 * i + h]))
            loads[-1].start()

    barrier = pltpu.get_barrier_semaphore()

    def greet(k, carry):
        pl.semaphore_signal(barrier, inc=1, device_id=peer(k)[1], device_id_type=MESH)
        return carry

    lax.fori_loop(1, chips, greet, 0)
    for dev in (partner, (row, z_up), (row, z_down)):
        pl.semaphore_signal(barrier, inc=1, device_id=dev, device_id_type=MESH)

    def gram_step(p, s):
        rs = pl.ds(pl.multiple_of(s * step_rows, step_rows), step_rows)
        lead, mate = xv[2 * p, rs, :], xv[2 * p + 1, rs, :]
        lh, ll = split(lead)
        mh, ml = split(mate)
        gram[p] += mm_t(lh, mh) + (mm_t(lh, ml) + mm_t(ll, mh))
        sq[p, 0] += jnp.sum((lead * lead).reshape(step_rows // 8, 8, BLK), axis=0)
        sq[p, 1] += jnp.sum((mate * mate).reshape(step_rows // 8, 8, BLK), axis=0)

    def squares(p):
        lead_sq = jnp.sum(sq[p, 0], axis=0, keepdims=True)
        mate_sq = jnp.sum(sq[p, 1], axis=0, keepdims=True)
        return jnp.concatenate(
            [lead_sq[:, :HALF], lead_sq[:, HALF:], mate_sq[:, :HALF], mate_sq[:, HALF:], jnp.zeros((4, HALF), f32)],
            axis=0,
        )

    def part_copy(rnd):
        return pltpu.make_async_remote_copy(
            part_send.at[rnd], part_recv.at[rnd], part_s.at[rnd], part_r.at[rnd], device_id=partner, device_id_type=MESH
        )

    def send_part(rnd):
        part_send[rnd, 0:BLK, :] = gram[other, :, 0:HALF]
        part_send[rnd, BLK : 2 * BLK, :] = gram[other, :, HALF:BLK]
        part_send[rnd, 2 * BLK : 2 * BLK + 8, :] = squares(other)
        part_copy(rnd).start()

    def reduce_gram(rnd):
        own_sq = squares(core)
        part_copy(rnd).wait()
        left = gram[core, :, 0:HALF] + part_recv[rnd, 0:BLK, :]
        right = gram[core, :, HALF:BLK] + part_recv[rnd, BLK : 2 * BLK, :]
        both_sq = own_sq + part_recv[rnd, 2 * BLK : 2 * BLK + 8, :]
        rs_src[rnd, :, 0:crow, :] = left.reshape(chips, crow, HALF)
        rs_src[rnd, :, crow : 2 * crow, :] = right.reshape(chips, crow, HALF)
        rs_src[rnd, :, 2 * crow : 2 * crow + 8, :] = jnp.broadcast_to(both_sq[None], (chips, 8, HALF))

        def rs_copy(k):
            t, dev = peer(k)
            return pltpu.make_async_remote_copy(
                rs_src.at[rnd, t], rs_recv.at[rnd, chip], rs_s.at[rnd, k], rs_r.at[rnd, chip],
                device_id=dev, device_id_type=MESH,
            )

        def ag_copy(k):
            _, dev = peer(k)
            return pltpu.make_async_remote_copy(
                ag.at[rnd, chip], ag.at[rnd, chip], ag_s.at[rnd, k], ag_r.at[rnd, chip],
                device_id=dev, device_id_type=MESH,
            )

        def rs_arrival(t):
            return pltpu.make_async_remote_copy(
                rs_src.at[rnd, t], rs_recv.at[rnd, t], rs_s.at[rnd, 0], rs_r.at[rnd, t],
                device_id=partner, device_id_type=MESH,
            )

        def ag_arrival(t):
            return pltpu.make_async_remote_copy(
                ag.at[rnd, t], ag.at[rnd, t], ag_s.at[rnd, 0], ag_r.at[rnd, t],
                device_id=partner, device_id_type=MESH,
            )

        def each(fn):
            def step(k, carry):
                fn(k)
                return carry

            lax.fori_loop(1, chips, step, 0)

        each(lambda k: rs_copy(k).start())
        rs_recv[rnd, chip] = rs_src[rnd, chip]
        each(lambda k: rs_arrival(peer(k)[0]).wait_recv())
        total = jnp.sum(rs_recv[rnd], axis=0)
        ag[rnd, chip] = total[0 : 2 * crow]
        each(lambda k: ag_copy(k).start())
        each(lambda k: rs_copy(k).wait_send())
        each(lambda k: ag_arrival(peer(k)[0]).wait_recv())
        each(lambda k: ag_copy(k).wait_send())
        return total[2 * crow : 2 * crow + 8]

    def rotation(rnd, sums):
        lead_sq = jnp.concatenate([sums[0:1], sums[1:2]], axis=1)
        mate_sq = jnp.concatenate([sums[2:3], sums[3:4]], axis=1)
        lead_col = jnp.broadcast_to(lead_sq, (8, BLK)).T[:, 0:1]
        cross = jnp.concatenate(
            [ag[rnd, :, 0:crow, :].reshape(BLK, HALF), ag[rnd, :, crow : 2 * crow, :].reshape(BLK, HALF)], axis=1
        )
        cmat[...] = cross / (lead_col + mate_sq + EPS)
        ident = eye()
        gmat[...] = ident + 0.25 * full(cmat[...], cmat[...], ((1,), (1,)))
        scale = 2.0 / (1.0 + BOUND)
        rx[0:BLK] = ident - scale * gmat[...]
        rx[BLK : 2 * BLK] = scale * ident

        def step(_, radius):
            s = 2.0 / (2.0 - radius * radius)
            hi, lo = split(rx[...])
            prod = mm3((hi, lo), (hi[0:BLK], lo[0:BLK]))
            rx[0:BLK] = s * prod[0:BLK] + (1.0 - s) * eye()
            rx[BLK : 2 * BLK] = s * (rx[BLK : 2 * BLK] + prod[BLK : 2 * BLK])
            return radius * radius / (2.0 - radius * radius)

        lax.fori_loop(0, STEPS, step, f32((BOUND - 1.0) / (BOUND + 1.0)))

        def correct(_, carry):
            x = rx[BLK : 2 * BLK]
            err = eye() - full(gmat[...], x, ((1,), (0,)))
            rx[BLK : 2 * BLK] = x + mm3(split(x), split(err))
            return carry

        lax.fori_loop(0, 2, correct, 0)
        inv = rx[BLK : 2 * BLK]
        w = full(inv, cmat[...], ((1,), (0,)))
        qv[rnd, core, 0] = 2.0 * inv - ident
        qv[rnd, core, 1] = w
        qv[rnd, core, 2] = ident - 0.5 * full(cmat[...], w, ((0,), (0,)))

    def q_copy(rnd, p):
        return pltpu.make_async_remote_copy(
            qv.at[rnd, p], qv.at[rnd, p], q_s.at[rnd], q_r.at[rnd], device_id=partner, device_id_type=MESH
        )

    def rotate(p, s):
        rs = pl.ds(pl.multiple_of(s * step_rows, step_rows), step_rows)
        x = jnp.concatenate([xv[2 * p, rs, :], xv[2 * p + 1, rs, :]], axis=1)
        xh, xl = split(x)
        for h in range(2):
            cols = slice(h * BLK, (h + 1) * BLK)
            nv[2 * p + h, rs, :] = mm3((xh, xl), (qhi[p, :, cols], qlo[p, :, cols]))

    def loop(n, fn):
        def step(s, carry):
            fn(s)
            return carry

        lax.fori_loop(0, n, step, 0)

    up_slot = down_slot = jnp.int32(0)
    for j in range(4):
        above, below = plan_ref[1, z_up * 4 + j], plan_ref[1, z_down * 4 + j]
        up_slot = jnp.where(above // 4 == z, above - 4 * z, up_slot)
        down_slot = jnp.where(below // 4 == z, below - 4 * z, down_slot)
    origin = [plan_ref[1, z * 4 + j] for j in range(4)]

    def z_copy(way, s):
        rs = pl.ds(s * step_rows, step_rows)
        return pltpu.make_async_remote_copy(
            zsend.at[way, rs, :], zrecv.at[way, rs, :], z_s.at[way, s], z_r.at[way, s],
            device_id=(row, z_up if way == 0 else z_down), device_id_type=MESH,
        )

    gram[...] = jnp.zeros_like(gram)
    sq[...] = jnp.zeros_like(sq)
    loads[0].wait()
    loads[1].wait()
    loop(n_steps, lambda s: gram_step(other, s))
    pl.semaphore_wait(barrier, chips + 2)
    send_part(0)
    loads[2].wait()
    loads[3].wait()
    loop(n_steps, lambda s: gram_step(core, s))
    rotation(0, reduce_gram(0))
    q_copy(0, core).start()
    put_rotation([qv[0, core, i] for i in range(3)], qhi, qlo, core)
    loop(n_steps, lambda s: rotate(core, s))
    q_copy(0, core).wait_send()
    q_copy(0, other).wait_recv()
    put_rotation([qv[0, other, i] for i in range(3)], qhi, qlo, other)
    for s in range(n_steps):
        rotate(other, s)
        rs = pl.ds(s * step_rows, step_rows)
        zsend[0, rs, :] = nv[up_slot, rs, :]
        z_copy(0, s).start()
        zsend[1, rs, :] = nv[down_slot, rs, :]
        z_copy(1, s).start()

    gram[...] = jnp.zeros_like(gram)
    sq[...] = jnp.zeros_like(sq)
    outs = []
    for s in range(n_steps):
        rs = pl.ds(s * step_rows, step_rows)
        z_copy(0, s).wait_recv()
        z_copy(1, s).wait_recv()
        for j in range(4):
            home = origin[j] // 4
            own = nv[jnp.clip(origin[j] - 4 * z, 0, 3), rs, :]
            xv[j, rs, :] = jnp.where(
                home == z, own, jnp.where(home < z, zrecv[0, rs, :], zrecv[1, rs, :])
            )
            outs.append(
                pltpu.make_async_copy(xv.at[j, rs, :], x2_ref.at[rs, j * BLK : (j + 1) * BLK], out_sem.at[s, j])
            )
            outs[-1].start()
        gram_step(other, s)
        if s == n_steps - 1:
            send_part(1)
        gram_step(core, s)
    for s in range(n_steps):
        z_copy(0, s).wait_send()
        z_copy(1, s).wait_send()
    rotation(1, reduce_gram(1))
    q_copy(1, core).start()
    for copy in outs:
        copy.wait()
    q_copy(1, core).wait_send()
    q_copy(1, other).wait_recv()
    final = pltpu.make_async_copy(qv.at[1], q_ref, load_sem.at[0])
    final.start()
    final.wait()


def two_rounds(plan, x, n_row, n_col):
    rows = x.shape[0]
    step_rows = rows // 4
    chips = n_row // 2
    crow = BLK // chips
    dma = pltpu.SemaphoreType.DMA
    return pl.pallas_call(
        functools.partial(rounds_kernel, n_row, n_col, rows, step_rows),
        out_shape=[jax.ShapeDtypeStruct(x.shape, f32), jax.ShapeDtypeStruct((2, 3, BLK, BLK), f32)],
        in_specs=[pl.BlockSpec(memory_space=pltpu.SMEM), pl.BlockSpec(memory_space=pl.ANY)],
        out_specs=[pl.BlockSpec(memory_space=pl.ANY)] * 2,
        scratch_shapes=[
            pltpu.VMEM((4, rows, BLK), f32),
            pltpu.VMEM((4, rows, BLK), f32),
            pltpu.VMEM((2, rows, BLK), f32),
            pltpu.VMEM((2, rows, BLK), f32),
            pltpu.VMEM((2, BLK, BLK), f32),
            pltpu.VMEM((2, 2, 8, BLK), f32),
            pltpu.VMEM((2, 2 * BLK + 8, HALF), f32),
            pltpu.VMEM((2, 2 * BLK + 8, HALF), f32),
            pltpu.VMEM((2, chips, 2 * crow + 8, HALF), f32),
            pltpu.VMEM((2, chips, 2 * crow + 8, HALF), f32),
            pltpu.VMEM((2, chips, 2 * crow, HALF), f32),
            pltpu.VMEM((2 * BLK, BLK), f32),
            pltpu.VMEM((BLK, BLK), f32),
            pltpu.VMEM((BLK, BLK), f32),
            pltpu.VMEM((2, 2, 3, BLK, BLK), f32),
            pltpu.VMEM((2, 2 * BLK, 2 * BLK), bf16),
            pltpu.VMEM((2, 2 * BLK, 2 * BLK), bf16),
            dma((4,)),
            dma((2,)), dma((2,)),
            dma((2, chips)), dma((2, chips)),
            dma((2, chips)), dma((2, chips)),
            dma((2,)), dma((2,)),
            dma((2, 4)), dma((2, 4)),
            dma((4, 4)),
        ],
        compiler_params=pltpu.CompilerParams(collective_id=0, has_side_effects=True, vmem_limit_bytes=56 << 20),
    )(plan, x)


def rotate_kernel(x_ref, q_ref, o_ref, qhi, qlo):
    @pl.when(pl.program_id(0) == 0)
    def _():
        for p in range(2):
            put_rotation([q_ref[p, i] for i in range(3)], qhi, qlo, p)

    for p in range(2):
        xh, xl = split(x_ref[:, 2 * p * BLK : (2 * p + 2) * BLK])
        for h in range(2):
            cols = slice(h * BLK, (h + 1) * BLK)
            o_ref[:, (2 * p + h) * BLK : (2 * p + h + 1) * BLK] = mm3(
                (xh, xl), (qhi[p, :, cols], qlo[p, :, cols])
            )


def last_rotation(x, q):
    rows = x.shape[0]
    step_rows = rows // 4
    return pl.pallas_call(
        rotate_kernel,
        grid=(rows // step_rows,),
        out_shape=jax.ShapeDtypeStruct(x.shape, f32),
        in_specs=[
            pl.BlockSpec((step_rows, 4 * BLK), lambda i: (i, 0)),
            pl.BlockSpec((2, 3, BLK, BLK), lambda i: (0, 0, 0, 0)),
        ],
        out_specs=pl.BlockSpec((step_rows, 4 * BLK), lambda i: (i, 0)),
        scratch_shapes=[pltpu.VMEM((2, 2 * BLK, 2 * BLK), bf16)] * 2,
        compiler_params=pltpu.CompilerParams(vmem_limit_bytes=48 << 20),
    )(x, q)


def shards(n_row, n_col, activations, plan):
    x2, q = two_rounds(plan, activations, n_row, n_col)
    return last_rotation(x2, q)


def solution(mesh):
    placed = (P("row", "col"), P())
    return jax.shard_map(
        functools.partial(shards, mesh.shape["row"], mesh.shape["col"]),
        mesh=mesh, in_specs=placed, out_specs=P("row", "col"), check_vma=False,
    )
```

```python
import functools
import math

import jax
import jax.numpy as jnp
from jax import lax
from jax.experimental import pallas as pl
from jax.experimental.pallas import tpu as pltpu
from jax.sharding import PartitionSpec as P

BLK = 256
HALF = 128
EPS = 1e-6
STEPS = 7
BOUND = 1.02 * (1.0 + (BLK / 2) ** 2 / 4)
MESH = pl.DeviceIdType.MESH
HIGHEST = lax.Precision.HIGHEST
f32, bf16 = jnp.float32, jnp.bfloat16


def split(value):
    hi = value.astype(bf16)
    return hi, (value - hi.astype(f32)).astype(bf16)


def mm(a, b):
    return lax.dot_general(a, b, (((1,), (0,)), ((), ())), preferred_element_type=f32)


def mm_t(a, b):
    return lax.dot_general(a, b, (((0,), (0,)), ((), ())), preferred_element_type=f32)


def mm3(a, b):
    return mm(a[0], b[0]) + (mm(a[0], b[1]) + mm(a[1], b[0]))


def full(a, b, dims):
    return lax.dot_general(a, b, (dims, ((), ())), precision=HIGHEST, preferred_element_type=f32)


def eye():
    rows = lax.broadcasted_iota(jnp.int32, (BLK, BLK), 0)
    cols = lax.broadcasted_iota(jnp.int32, (BLK, BLK), 1)
    return jnp.where(rows == cols, 1.0, 0.0).astype(f32)


def put_rotation(q, hi_ref, lo_ref, pair):
    q11, w, q22 = q
    for value, r, c in ((q11, 0, 0), (w, 0, 1), (-w.T, 1, 0), (q22, 1, 1)):
        hi, lo = split(value)
        hi_ref[pair, r * BLK : (r + 1) * BLK, c * BLK : (c + 1) * BLK] = hi
        lo_ref[pair, r * BLK : (r + 1) * BLK, c * BLK : (c + 1) * BLK] = lo


def rounds_kernel(
    n_row, n_col, rows, step_rows,
    plan_ref, x_ref, x2_ref, q_ref,
    xv, nv, zsend, zrecv, gram, sq, part_send, part_recv, rs_src, rs_recv, ag, gmat, cmat, qv, qhi, qlo,
    load_sem, part_s, part_r, rs_s, rs_r, ag_s, ag_r, q_s, q_r, z_s, z_r, out_sem,
):
    chips = n_row // 2
    crow = BLK // chips
    row, z = lax.axis_index("row"), lax.axis_index("col")
    core, chip = lax.rem(row, 2), row // 2
    other = 1 - core
    partner = (chip * 2 + other, z)
    z_up, z_down = lax.rem(z + 1, n_col), lax.rem(z + n_col - 1, n_col)
    n_steps = rows // step_rows

    side = math.isqrt(chips)
    cx, cy = chip // side, lax.rem(chip, side)

    def hops(offset):
        return min(offset, side - offset)

    far_first = sorted(
        [(dx, dy) for dx in range(side) for dy in range(side) if (dx, dy) != (0, 0)],
        key=lambda d: -hops(d[0]) - hops(d[1]),
    )
    peers = []
    for dx, dy in far_first:
        t = lax.rem(cx + dx, side) * side + lax.rem(cy + dy, side)
        peers.append((t, (t * 2 + core, z)))

    loads = []
    for i, p in enumerate((other, core)):
        for h in range(2):
            cols = pl.ds(pl.multiple_of((2 * p + h) * BLK, BLK), BLK)
            loads.append(pltpu.make_async_copy(x_ref.at[:, cols], xv.at[2 * p + h], load_sem.at[2 * i + h]))
            loads[-1].start()

    barrier = pltpu.get_barrier_semaphore()

    for dev in [dev for _, dev in peers] + [(row, z_up), (row, z_down), partner]:
        pl.semaphore_signal(barrier, inc=1, device_id=dev, device_id_type=MESH)

    def gram_step(p, s):
        rs = pl.ds(pl.multiple_of(s * step_rows, step_rows), step_rows)
        lead, mate = xv[2 * p, rs, :], xv[2 * p + 1, rs, :]
        lh, ll = split(lead)
        mh, ml = split(mate)
        gram[p] += mm_t(lh, mh) + (mm_t(lh, ml) + mm_t(ll, mh))
        sq[p, 0] += jnp.sum((lead * lead).reshape(step_rows // 8, 8, BLK), axis=0)
        sq[p, 1] += jnp.sum((mate * mate).reshape(step_rows // 8, 8, BLK), axis=0)

    def squares(p):
        lead_sq = jnp.sum(sq[p, 0], axis=0, keepdims=True)
        mate_sq = jnp.sum(sq[p, 1], axis=0, keepdims=True)
        return jnp.concatenate(
            [lead_sq[:, :HALF], lead_sq[:, HALF:], mate_sq[:, :HALF], mate_sq[:, HALF:], jnp.zeros((4, HALF), f32)],
            axis=0,
        )

    def part_copy(rnd):
        return pltpu.make_async_remote_copy(
            part_send.at[rnd], part_recv.at[rnd], part_s.at[rnd], part_r.at[rnd], device_id=partner, device_id_type=MESH
        )

    def send_part(rnd):
        part_send[rnd, 0:BLK, :] = gram[other, :, 0:HALF]
        part_send[rnd, BLK : 2 * BLK, :] = gram[other, :, HALF:BLK]
        part_send[rnd, 2 * BLK : 2 * BLK + 8, :] = squares(other)
        part_copy(rnd).start()

    def reduce_gram(rnd):
        own_sq = squares(core)
        part_copy(rnd).wait()
        left = gram[core, :, 0:HALF] + part_recv[rnd, 0:BLK, :]
        right = gram[core, :, HALF:BLK] + part_recv[rnd, BLK : 2 * BLK, :]
        both_sq = own_sq + part_recv[rnd, 2 * BLK : 2 * BLK + 8, :]
        rs_src[rnd, :, 0:crow, :] = left.reshape(chips, crow, HALF)
        rs_src[rnd, :, crow : 2 * crow, :] = right.reshape(chips, crow, HALF)
        rs_src[rnd, :, 2 * crow : 2 * crow + 8, :] = jnp.broadcast_to(both_sq[None], (chips, 8, HALF))

        sent = crow * 2 + 4

        def rs_copy(k, t, dev, source):
            return pltpu.make_async_remote_copy(
                rs_src.at[rnd, t, 0:sent], rs_recv.at[rnd, source, 0:sent], rs_s.at[rnd, k], rs_r.at[rnd, source],
                device_id=dev, device_id_type=MESH,
            )

        def ag_copy(k, dev, source):
            return pltpu.make_async_remote_copy(
                ag.at[rnd, source], ag.at[rnd, source], ag_s.at[rnd, k], ag_r.at[rnd, source],
                device_id=dev, device_id_type=MESH,
            )

        for k, (t, dev) in enumerate(peers):
            rs_copy(k, t, dev, chip).start()
        rs_recv[rnd, chip] = rs_src[rnd, chip]
        for k, (t, dev) in enumerate(peers):
            rs_copy(k, t, dev, t).wait_recv()
        total = jnp.sum(rs_recv[rnd], axis=0)
        ag[rnd, chip] = total[0 : 2 * crow]
        for k, (t, dev) in enumerate(peers):
            ag_copy(k, dev, chip).start()
        for k, (t, dev) in enumerate(peers):
            rs_copy(k, t, dev, chip).wait_send()
        for k, (t, dev) in enumerate(peers):
            ag_copy(k, dev, t).wait_recv()
        for k, (t, dev) in enumerate(peers):
            ag_copy(k, dev, chip).wait_send()
        return total[2 * crow : 2 * crow + 8]

    def rotation(rnd, sums):
        lead_sq = jnp.concatenate([sums[0:1], sums[1:2]], axis=1)
        mate_sq = jnp.concatenate([sums[2:3], sums[3:4]], axis=1)
        lead_col = jnp.broadcast_to(lead_sq, (8, BLK)).T[:, 0:1]
        cross = jnp.concatenate(
            [ag[rnd, :, 0:crow, :].reshape(BLK, HALF), ag[rnd, :, crow : 2 * crow, :].reshape(BLK, HALF)], axis=1
        )
        cmat[...] = cross / (lead_col + mate_sq + EPS)
        ident = eye()
        gmat[...] = ident + 0.25 * full(cmat[...], cmat[...], ((1,), (1,)))
        scale = 2.0 / (1.0 + BOUND)
        radius = (BOUND - 1.0) / (BOUND + 1.0)
        res = split(ident - scale * gmat[...])
        inv = None
        for k in range(STEPS):
            s = 2.0 / (2.0 - radius * radius)
            radius = radius * radius / (2.0 - radius * radius)
            if k < STEPS - 1:
                square = mm3(res, res)
            if k == 0:
                inv = (s * scale) * (ident + (res[0].astype(f32) + res[1].astype(f32)))
            else:
                inv = s * (inv + mm3(split(inv), res))
            if k < STEPS - 1:
                res = split(s * square + (1.0 - s) * ident)
        inv_parts = split(inv)
        inv = inv + mm3(inv_parts, split(ident - mm3(split(gmat[...]), inv_parts)))
        inv = inv + mm3(split(inv), split(ident - full(gmat[...], inv, ((1,), (0,)))))
        w = full(inv, cmat[...], ((1,), (0,)))
        qv[rnd, core, 0] = 2.0 * inv - ident
        qv[rnd, core, 1] = w
        qv[rnd, core, 2] = ident - 0.5 * full(cmat[...], w, ((0,), (0,)))

    def q_copy(rnd, p):
        return pltpu.make_async_remote_copy(
            qv.at[rnd, p], qv.at[rnd, p], q_s.at[rnd], q_r.at[rnd], device_id=partner, device_id_type=MESH
        )

    def q_out(p):
        return pltpu.make_async_remote_copy(
            qv.at[1, p], q_ref.at[p], q_s.at[1], q_r.at[1], device_id=partner, device_id_type=MESH
        )

    def rotate(p, s):
        rs = pl.ds(pl.multiple_of(s * step_rows, step_rows), step_rows)
        x = jnp.concatenate([xv[2 * p, rs, :], xv[2 * p + 1, rs, :]], axis=1)
        xh, xl = split(x)
        for h in range(2):
            cols = slice(h * BLK, (h + 1) * BLK)
            nv[2 * p + h, rs, :] = mm3((xh, xl), (qhi[p, :, cols], qlo[p, :, cols]))

    def loop(n, fn):
        def step(s, carry):
            fn(s)
            return carry

        lax.fori_loop(0, n, step, 0)

    up_slot = down_slot = jnp.int32(0)
    for j in range(4):
        above, below = plan_ref[1, z_up * 4 + j], plan_ref[1, z_down * 4 + j]
        up_slot = jnp.where(above // 4 == z, above - 4 * z, up_slot)
        down_slot = jnp.where(below // 4 == z, below - 4 * z, down_slot)
    origin = [plan_ref[1, z * 4 + j] for j in range(4)]

    def z_copy(way, s):
        rs = pl.ds(s * step_rows, step_rows)
        return pltpu.make_async_remote_copy(
            zsend.at[way, rs, :], zrecv.at[way, rs, :], z_s.at[way, s], z_r.at[way, s],
            device_id=(row, z_up if way == 0 else z_down), device_id_type=MESH,
        )

    gram[...] = jnp.zeros_like(gram)
    sq[...] = jnp.zeros_like(sq)
    loads[0].wait()
    loads[1].wait()
    loop(n_steps, lambda s: gram_step(other, s))
    pl.semaphore_wait(barrier, chips + 2)
    send_part(0)
    loads[2].wait()
    loads[3].wait()
    loop(n_steps, lambda s: gram_step(core, s))
    rotation(0, reduce_gram(0))
    q_copy(0, core).start()
    put_rotation([qv[0, core, i] for i in range(3)], qhi, qlo, core)
    loop(n_steps, lambda s: rotate(core, s))
    q_copy(0, core).wait_send()
    q_copy(0, other).wait_recv()
    put_rotation([qv[0, other, i] for i in range(3)], qhi, qlo, other)
    for s in range(n_steps):
        rotate(other, s)
        rs = pl.ds(s * step_rows, step_rows)
        zsend[0, rs, :] = nv[up_slot, rs, :]
        z_copy(0, s).start()
        zsend[1, rs, :] = nv[down_slot, rs, :]
        z_copy(1, s).start()

    gram[...] = jnp.zeros_like(gram)
    sq[...] = jnp.zeros_like(sq)
    outs = []
    for s in range(n_steps):
        rs = pl.ds(s * step_rows, step_rows)
        z_copy(0, s).wait_recv()
        z_copy(1, s).wait_recv()
        for j in range(4):
            home = origin[j] // 4
            own = nv[jnp.clip(origin[j] - 4 * z, 0, 3), rs, :]
            xv[j, rs, :] = jnp.where(
                home == z, own, jnp.where(home < z, zrecv[0, rs, :], zrecv[1, rs, :])
            )
            outs.append(
                pltpu.make_async_copy(xv.at[j, rs, :], x2_ref.at[rs, j * BLK : (j + 1) * BLK], out_sem.at[s, j])
            )
            outs[-1].start()
        gram_step(other, s)
        if s == n_steps - 1:
            send_part(1)
        gram_step(core, s)
    for s in range(n_steps):
        z_copy(0, s).wait_send()
        z_copy(1, s).wait_send()
    rotation(1, reduce_gram(1))
    q_out(core).start()
    final = pltpu.make_async_copy(qv.at[1, core], q_ref.at[core], load_sem.at[0])
    final.start()
    for copy in outs:
        copy.wait()
    final.wait()
    q_out(core).wait_send()
    q_out(other).wait_recv()


def two_rounds(plan, x, n_row, n_col):
    rows = x.shape[0]
    step_rows = rows // 4
    chips = n_row // 2
    crow = BLK // chips
    dma = pltpu.SemaphoreType.DMA
    return pl.pallas_call(
        functools.partial(rounds_kernel, n_row, n_col, rows, step_rows),
        out_shape=[jax.ShapeDtypeStruct(x.shape, f32), jax.ShapeDtypeStruct((2, 3, BLK, BLK), f32)],
        in_specs=[pl.BlockSpec(memory_space=pltpu.SMEM), pl.BlockSpec(memory_space=pl.ANY)],
        out_specs=[pl.BlockSpec(memory_space=pl.ANY)] * 2,
        scratch_shapes=[
            pltpu.VMEM((4, rows, BLK), f32),
            pltpu.VMEM((4, rows, BLK), f32),
            pltpu.VMEM((2, rows, BLK), f32),
            pltpu.VMEM((2, rows, BLK), f32),
            pltpu.VMEM((2, BLK, BLK), f32),
            pltpu.VMEM((2, 2, 8, BLK), f32),
            pltpu.VMEM((2, 2 * BLK + 8, HALF), f32),
            pltpu.VMEM((2, 2 * BLK + 8, HALF), f32),
            pltpu.VMEM((2, chips, 2 * crow + 8, HALF), f32),
            pltpu.VMEM((2, chips, 2 * crow + 8, HALF), f32),
            pltpu.VMEM((2, chips, 2 * crow, HALF), f32),
            pltpu.VMEM((BLK, BLK), f32),
            pltpu.VMEM((BLK, BLK), f32),
            pltpu.VMEM((2, 2, 3, BLK, BLK), f32),
            pltpu.VMEM((2, 2 * BLK, 2 * BLK), bf16),
            pltpu.VMEM((2, 2 * BLK, 2 * BLK), bf16),
            dma((4,)),
            dma((2,)), dma((2,)),
            dma((2, chips)), dma((2, chips)),
            dma((2, chips)), dma((2, chips)),
            dma((2,)), dma((2,)),
            dma((2, 4)), dma((2, 4)),
            dma((4, 4)),
        ],
        compiler_params=pltpu.CompilerParams(collective_id=0, has_side_effects=True, vmem_limit_bytes=56 << 20),
    )(plan, x)


def rotate_kernel(x_ref, q_ref, o_ref, qhi, qlo):
    @pl.when(pl.program_id(0) == 0)
    def _():
        for p in range(2):
            put_rotation([q_ref[p, i] for i in range(3)], qhi, qlo, p)

    for p in range(2):
        xh, xl = split(x_ref[:, 2 * p * BLK : (2 * p + 2) * BLK])
        for h in range(2):
            cols = slice(h * BLK, (h + 1) * BLK)
            o_ref[:, (2 * p + h) * BLK : (2 * p + h + 1) * BLK] = mm3(
                (xh, xl), (qhi[p, :, cols], qlo[p, :, cols])
            )


def last_rotation(x, q):
    rows = x.shape[0]
    step_rows = rows // 4
    return pl.pallas_call(
        rotate_kernel,
        grid=(rows // step_rows,),
        out_shape=jax.ShapeDtypeStruct(x.shape, f32),
        in_specs=[
            pl.BlockSpec((step_rows, 4 * BLK), lambda i: (i, 0)),
            pl.BlockSpec((2, 3, BLK, BLK), lambda i: (0, 0, 0, 0)),
        ],
        out_specs=pl.BlockSpec((step_rows, 4 * BLK), lambda i: (i, 0)),
        scratch_shapes=[pltpu.VMEM((2, 2 * BLK, 2 * BLK), bf16)] * 2,
        compiler_params=pltpu.CompilerParams(vmem_limit_bytes=60 << 20),
    )(x, q)


def shards(n_row, n_col, activations, plan):
    x2, q = two_rounds(plan, activations, n_row, n_col)
    return last_rotation(x2, q)


def solution(mesh):
    placed = (P("row", "col"), P())
    return jax.shard_map(
        functools.partial(shards, mesh.shape["row"], mesh.shape["col"]),
        mesh=mesh, in_specs=placed, out_specs=P("row", "col"), check_vma=False,
    )
```

```python
import functools
import math

import jax
import jax.numpy as jnp
from jax import lax
from jax.experimental import pallas as pl
from jax.experimental.pallas import tpu as pltpu
from jax.sharding import PartitionSpec as P

BLK = 256
HALF = 128
EPS = 1e-6
STEPS = 7
BOUND = 1.02 * (1.0 + (BLK / 2) ** 2 / 4)
MESH = pl.DeviceIdType.MESH
HIGHEST = lax.Precision.HIGHEST
f32, bf16 = jnp.float32, jnp.bfloat16


def split(value):
    hi = value.astype(bf16)
    return hi, (value - hi.astype(f32)).astype(bf16)


def mm(a, b):
    return lax.dot_general(a, b, (((1,), (0,)), ((), ())), preferred_element_type=f32)


def mm_t(a, b):
    return lax.dot_general(a, b, (((0,), (0,)), ((), ())), preferred_element_type=f32)


def mm3(a, b):
    return mm(a[0], b[0]) + (mm(a[0], b[1]) + mm(a[1], b[0]))


def full(a, b, dims):
    return lax.dot_general(a, b, (dims, ((), ())), precision=HIGHEST, preferred_element_type=f32)


def eye():
    rows = lax.broadcasted_iota(jnp.int32, (BLK, BLK), 0)
    cols = lax.broadcasted_iota(jnp.int32, (BLK, BLK), 1)
    return jnp.where(rows == cols, 1.0, 0.0).astype(f32)


def put_rotation(q, hi_ref, lo_ref, pair, whole_ref=None):
    q11, w, q22 = q
    for value, r, c in ((q11, 0, 0), (w, 0, 1), (-w.T, 1, 0), (q22, 1, 1)):
        hi, lo = split(value)
        hi_ref[pair, r * BLK : (r + 1) * BLK, c * BLK : (c + 1) * BLK] = hi
        lo_ref[pair, r * BLK : (r + 1) * BLK, c * BLK : (c + 1) * BLK] = lo
        if whole_ref is not None:
            whole_ref[2 * pair + c, r] = value


def rounds_kernel(
    n_row, n_col, rows,
    plan_ref, x_ref, x2_ref, q_ref,
    xv, nv, zsend, zrecv, gram, sq, part_send, part_recv, rs_src, rs_recv, ag, gmat, cmat, qv, qhi, qlo, qf,
    esend, erecv, zearly, qz, qz_all, qz_other,
    load_sem, part_s, part_r, rs_s, rs_r, ag_s, ag_r, q_s, q_r, z_s, z_r, out_sem,
    e_s, e_r, qz_s, qz_r, qa_s, qa_r, qp_s, qp_r,
):
    chips = n_row // 2
    crow = BLK // chips
    row, z = lax.axis_index("row"), lax.axis_index("col")
    core, chip = lax.rem(row, 2), row // 2
    other = 1 - core
    partner = (chip * 2 + other, z)
    z_up, z_down = lax.rem(z + 1, n_col), lax.rem(z + n_col - 1, n_col)
    unit = rows // 8
    late = [(0, 2 * unit), (2 * unit, 2 * unit), (4 * unit, unit)]
    early, n_early = 5 * unit, 3 * unit

    side = math.isqrt(chips)
    cx, cy = chip // side, lax.rem(chip, side)

    def hops(offset):
        return min(offset, side - offset)

    far_first = sorted(
        [(dx, dy) for dx in range(side) for dy in range(side) if (dx, dy) != (0, 0)],
        key=lambda d: -hops(d[0]) - hops(d[1]),
    )
    peers = []
    for dx, dy in far_first:
        t = lax.rem(cx + dx, side) * side + lax.rem(cy + dy, side)
        peers.append((t, (t * 2 + core, z)))

    loads = []
    for i, p in enumerate((other, core)):
        for h in range(2):
            cols = pl.ds(pl.multiple_of((2 * p + h) * BLK, BLK), BLK)
            loads.append(pltpu.make_async_copy(x_ref.at[:, cols], xv.at[2 * p + h], load_sem.at[2 * i + h]))
            loads[-1].start()

    barrier = pltpu.get_barrier_semaphore()

    for dev in [dev for _, dev in peers] + [(row, z_up), (row, z_down), partner]:
        pl.semaphore_signal(barrier, inc=1, device_id=dev, device_id_type=MESH)

    def gram_step(p, start, step_rows):
        rs = pl.ds(start, step_rows)
        lead, mate = xv[2 * p, rs, :], xv[2 * p + 1, rs, :]
        lh, ll = split(lead)
        mh, ml = split(mate)
        gram[p] += mm_t(lh, mh) + (mm_t(lh, ml) + mm_t(ll, mh))
        sq[p, 0] += jnp.sum((lead * lead).reshape(step_rows // 8, 8, BLK), axis=0)
        sq[p, 1] += jnp.sum((mate * mate).reshape(step_rows // 8, 8, BLK), axis=0)

    def squares(p):
        lead_sq = jnp.sum(sq[p, 0], axis=0, keepdims=True)
        mate_sq = jnp.sum(sq[p, 1], axis=0, keepdims=True)
        return jnp.concatenate(
            [lead_sq[:, :HALF], lead_sq[:, HALF:], mate_sq[:, :HALF], mate_sq[:, HALF:], jnp.zeros((4, HALF), f32)],
            axis=0,
        )

    def part_copy(rnd):
        return pltpu.make_async_remote_copy(
            part_send.at[rnd], part_recv.at[rnd], part_s.at[rnd], part_r.at[rnd], device_id=partner, device_id_type=MESH
        )

    def send_part(rnd):
        part_send[rnd, 0:BLK, :] = gram[other, :, 0:HALF]
        part_send[rnd, BLK : 2 * BLK, :] = gram[other, :, HALF:BLK]
        part_send[rnd, 2 * BLK : 2 * BLK + 8, :] = squares(other)
        part_copy(rnd).start()

    def reduce_gram(rnd):
        own_sq = squares(core)
        part_copy(rnd).wait()
        left = gram[core, :, 0:HALF] + part_recv[rnd, 0:BLK, :]
        right = gram[core, :, HALF:BLK] + part_recv[rnd, BLK : 2 * BLK, :]
        both_sq = own_sq + part_recv[rnd, 2 * BLK : 2 * BLK + 8, :]
        rs_src[rnd, :, 0:crow, :] = left.reshape(chips, crow, HALF)
        rs_src[rnd, :, crow : 2 * crow, :] = right.reshape(chips, crow, HALF)
        rs_src[rnd, :, 2 * crow : 2 * crow + 8, :] = jnp.broadcast_to(both_sq[None], (chips, 8, HALF))

        sent = crow * 2 + 4

        def rs_copy(k, t, dev, source):
            return pltpu.make_async_remote_copy(
                rs_src.at[rnd, t, 0:sent], rs_recv.at[rnd, source, 0:sent], rs_s.at[rnd, k], rs_r.at[rnd, source],
                device_id=dev, device_id_type=MESH,
            )

        def ag_copy(k, dev, source):
            return pltpu.make_async_remote_copy(
                ag.at[rnd, source], ag.at[rnd, source], ag_s.at[rnd, k], ag_r.at[rnd, source],
                device_id=dev, device_id_type=MESH,
            )

        for k, (t, dev) in enumerate(peers):
            rs_copy(k, t, dev, chip).start()
        rs_recv[rnd, chip] = rs_src[rnd, chip]
        for k, (t, dev) in enumerate(peers):
            rs_copy(k, t, dev, t).wait_recv()
        total = jnp.sum(rs_recv[rnd], axis=0)
        ag[rnd, chip] = total[0 : 2 * crow]
        for k, (t, dev) in enumerate(peers):
            ag_copy(k, dev, chip).start()
        for k, (t, dev) in enumerate(peers):
            rs_copy(k, t, dev, chip).wait_send()
        for k, (t, dev) in enumerate(peers):
            ag_copy(k, dev, t).wait_recv()
        for k, (t, dev) in enumerate(peers):
            ag_copy(k, dev, chip).wait_send()
        return total[2 * crow : 2 * crow + 8]

    def rotation(rnd, sums):
        lead_sq = jnp.concatenate([sums[0:1], sums[1:2]], axis=1)
        mate_sq = jnp.concatenate([sums[2:3], sums[3:4]], axis=1)
        lead_col = jnp.broadcast_to(lead_sq, (8, BLK)).T[:, 0:1]
        cross = jnp.concatenate(
            [ag[rnd, :, 0:crow, :].reshape(BLK, HALF), ag[rnd, :, crow : 2 * crow, :].reshape(BLK, HALF)], axis=1
        )
        cmat[...] = cross / (lead_col + mate_sq + EPS)
        ident = eye()
        gmat[...] = ident + 0.25 * full(cmat[...], cmat[...], ((1,), (1,)))
        scale = 2.0 / (1.0 + BOUND)
        radius = (BOUND - 1.0) / (BOUND + 1.0)
        res = split(ident - scale * gmat[...])
        inv = None
        for k in range(STEPS):
            s = 2.0 / (2.0 - radius * radius)
            radius = radius * radius / (2.0 - radius * radius)
            if k < STEPS - 1:
                square = mm3(res, res)
            if k == 0:
                inv = (s * scale) * (ident + (res[0].astype(f32) + res[1].astype(f32)))
            else:
                inv = s * (inv + mm3(split(inv), res))
            if k < STEPS - 1:
                res = split(s * square + (1.0 - s) * ident)
        inv_parts = split(inv)
        inv = inv + mm3(inv_parts, split(ident - mm3(split(gmat[...]), inv_parts)))
        inv = inv + mm3(split(inv), split(ident - full(gmat[...], inv, ((1,), (0,)))))
        w = full(inv, cmat[...], ((1,), (0,)))
        qv[rnd, core, 0] = 2.0 * inv - ident
        qv[rnd, core, 1] = w
        qv[rnd, core, 2] = ident - 0.5 * full(cmat[...], w, ((0,), (0,)))

    def q_copy(rnd, p):
        return pltpu.make_async_remote_copy(
            qv.at[rnd, p], qv.at[rnd, p], q_s.at[rnd], q_r.at[rnd], device_id=partner, device_id_type=MESH
        )

    def q_out(p):
        return pltpu.make_async_remote_copy(
            qv.at[1, p], q_ref.at[p], q_s.at[1], q_r.at[1], device_id=partner, device_id_type=MESH
        )

    def rotate(p, start, step_rows):
        rs = pl.ds(start, step_rows)
        x = jnp.concatenate([xv[2 * p, rs, :], xv[2 * p + 1, rs, :]], axis=1)
        xh, xl = split(x)
        for h in range(2):
            cols = slice(h * BLK, (h + 1) * BLK)
            nv[2 * p + h, rs, :] = mm3((xh, xl), (qhi[p, :, cols], qlo[p, :, cols]))

    up_slot = down_slot = jnp.int32(0)
    for j in range(4):
        above, below = plan_ref[1, z_up * 4 + j], plan_ref[1, z_down * 4 + j]
        up_slot = jnp.where(above // 4 == z, above - 4 * z, up_slot)
        down_slot = jnp.where(below // 4 == z, below - 4 * z, down_slot)
    origin = [plan_ref[1, z * 4 + j] for j in range(4)]

    def z_copy(way, i):
        rs = pl.ds(*late[i])
        return pltpu.make_async_remote_copy(
            zsend.at[way, rs, :], zrecv.at[way, rs, :], z_s.at[way, i], z_r.at[way, i],
            device_id=(row, z_up if way == 0 else z_down), device_id_type=MESH,
        )

    def early_copy(way):
        return pltpu.make_async_remote_copy(
            esend.at[way], erecv.at[way], e_s.at[way], e_r.at[way],
            device_id=(row, z_up if way == 0 else z_down), device_id_type=MESH,
        )

    def share_copy(way):
        return pltpu.make_async_remote_copy(
            qz.at[way], qz_all.at[chip, way], qz_s.at[way], qz_r.at[way],
            device_id=(row, z_up if way == 0 else z_down), device_id_type=MESH,
        )

    def share_gather(k, dev, source):
        return pltpu.make_async_remote_copy(
            qz_all.at[source], qz_all.at[source], qa_s.at[k], qa_r.at[source], device_id=dev, device_id_type=MESH
        )

    def share_swap():
        return pltpu.make_async_remote_copy(
            qz_all, qz_other, qp_s.at[0], qp_r.at[0], device_id=partner, device_id_type=MESH
        )

    gram[...] = jnp.zeros_like(gram)
    sq[...] = jnp.zeros_like(sq)
    loads[0].wait()
    loads[1].wait()
    for start in range(0, rows, 2 * unit):
        gram_step(other, start, 2 * unit)
    loads[2].wait()
    loads[3].wait()
    pl.semaphore_wait(barrier, chips + 2)
    send_part(0)
    for way, slot in enumerate((up_slot, down_slot)):
        for h in range(2):
            esend[way, h] = xv[(slot // 2) * 2 + h, pl.ds(early, n_early), :]
        early_copy(way).start()
    for start in range(0, rows, 2 * unit):
        gram_step(core, start, 2 * unit)
    rotation(0, reduce_gram(0))
    q_copy(0, core).start()
    put_rotation([qv[0, core, i] for i in range(3)], qhi, qlo, core, qf)
    for start, size in late:
        rotate(core, start, size)
    q_copy(0, core).wait_send()
    q_copy(0, other).wait_recv()
    put_rotation([qv[0, other, i] for i in range(3)], qhi, qlo, other, qf)
    for way, slot in enumerate((up_slot, down_slot)):
        qz[way] = qf[slot, core, pl.ds(pl.multiple_of(chip * crow, crow), crow), :]
        share_copy(way).start()
    for i, (start, size) in enumerate(late):
        rotate(other, start, size)
        rs = pl.ds(start, size)
        zsend[0, rs, :] = nv[up_slot, rs, :]
        z_copy(0, i).start()
        zsend[1, rs, :] = nv[down_slot, rs, :]
        z_copy(1, i).start()
    for way in range(2):
        share_copy(way).wait_recv()
    for k, (_, dev) in enumerate(peers):
        share_gather(k, dev, chip).start()
    rotate(core, early, n_early)
    rotate(other, early, n_early)

    gram[...] = jnp.zeros_like(gram)
    sq[...] = jnp.zeros_like(sq)
    outs = []

    def place(start, size, lower, upper):
        rs = pl.ds(start, size)
        for j in range(4):
            home = origin[j] // 4
            own = nv[jnp.clip(origin[j] - 4 * z, 0, 3), rs, :]
            xv[j, rs, :] = jnp.where(home == z, own, jnp.where(home < z, lower[...], upper[...]))
            outs.append(
                pltpu.make_async_copy(
                    xv.at[j, rs, :], x2_ref.at[rs, j * BLK : (j + 1) * BLK], out_sem.at[len(outs)]
                )
            )
            outs[-1].start()

    def arrive(i):
        z_copy(0, i).wait_recv()
        z_copy(1, i).wait_recv()
        rs = pl.ds(*late[i])
        place(*late[i], zrecv.at[0, rs, :], zrecv.at[1, rs, :])

    arrive(0)
    gram_step(other, *late[0])
    gram_step(core, *late[0])
    for k, (t, dev) in enumerate(peers):
        share_gather(k, dev, t).wait_recv()
    share_swap().start()
    for way in range(2):
        early_copy(way).wait_recv()
    for way in range(2):
        part = qz_all[:, way].reshape(BLK, BLK)
        zearly[way] = mm3(split(erecv[way, core]), split(part))
    share_swap().wait_recv()
    for way in range(2):
        part = qz_other[:, way].reshape(BLK, BLK)
        zearly[way] += mm3(split(erecv[way, other]), split(part))
    place(early, n_early, zearly.at[0], zearly.at[1])
    gram_step(other, early, n_early)
    gram_step(core, early, n_early)
    arrive(1)
    gram_step(other, *late[1])
    gram_step(core, *late[1])
    arrive(2)
    gram_step(other, *late[2])
    send_part(1)
    gram_step(core, *late[2])
    for way in range(2):
        for i in range(len(late)):
            z_copy(way, i).wait_send()
        early_copy(way).wait_send()
        share_copy(way).wait_send()
    for k, (_, dev) in enumerate(peers):
        share_gather(k, dev, chip).wait_send()
    share_swap().wait_send()
    rotation(1, reduce_gram(1))
    q_out(core).start()
    final = pltpu.make_async_copy(qv.at[1, core], q_ref.at[core], load_sem.at[0])
    final.start()
    for copy in outs:
        copy.wait()
    final.wait()
    q_out(core).wait_send()
    q_out(other).wait_recv()


def two_rounds(plan, x, n_row, n_col):
    rows = x.shape[0]
    n_early = 3 * rows // 8
    chips = n_row // 2
    crow = BLK // chips
    dma = pltpu.SemaphoreType.DMA
    return pl.pallas_call(
        functools.partial(rounds_kernel, n_row, n_col, rows),
        out_shape=[jax.ShapeDtypeStruct(x.shape, f32), jax.ShapeDtypeStruct((2, 3, BLK, BLK), f32)],
        in_specs=[pl.BlockSpec(memory_space=pltpu.SMEM), pl.BlockSpec(memory_space=pl.ANY)],
        out_specs=[pl.BlockSpec(memory_space=pl.ANY)] * 2,
        scratch_shapes=[
            pltpu.VMEM((4, rows, BLK), f32),
            pltpu.VMEM((4, rows, BLK), f32),
            pltpu.VMEM((2, rows, BLK), f32),
            pltpu.VMEM((2, rows, BLK), f32),
            pltpu.VMEM((2, BLK, BLK), f32),
            pltpu.VMEM((2, 2, 8, BLK), f32),
            pltpu.VMEM((2, 2 * BLK + 8, HALF), f32),
            pltpu.VMEM((2, 2 * BLK + 8, HALF), f32),
            pltpu.VMEM((2, chips, 2 * crow + 8, HALF), f32),
            pltpu.VMEM((2, chips, 2 * crow + 8, HALF), f32),
            pltpu.VMEM((2, chips, 2 * crow, HALF), f32),
            pltpu.VMEM((BLK, BLK), f32),
            pltpu.VMEM((BLK, BLK), f32),
            pltpu.VMEM((2, 2, 3, BLK, BLK), f32),
            pltpu.VMEM((2, 2 * BLK, 2 * BLK), bf16),
            pltpu.VMEM((2, 2 * BLK, 2 * BLK), bf16),
            pltpu.VMEM((4, 2, BLK, BLK), f32),
            pltpu.VMEM((2, 2, n_early, BLK), f32),
            pltpu.VMEM((2, 2, n_early, BLK), f32),
            pltpu.VMEM((2, n_early, BLK), f32),
            pltpu.VMEM((2, crow, BLK), f32),
            pltpu.VMEM((chips, 2, crow, BLK), f32),
            pltpu.VMEM((chips, 2, crow, BLK), f32),
            dma((4,)),
            dma((2,)), dma((2,)),
            dma((2, chips)), dma((2, chips)),
            dma((2, chips)), dma((2, chips)),
            dma((2,)), dma((2,)),
            dma((2, 3)), dma((2, 3)),
            dma((16,)),
            dma((2,)), dma((2,)),
            dma((2,)), dma((2,)),
            dma((chips,)), dma((chips,)),
            dma((1,)), dma((1,)),
        ],
        compiler_params=pltpu.CompilerParams(collective_id=0, has_side_effects=True, vmem_limit_bytes=56 << 20),
    )(plan, x)


def rotate_kernel(x_ref, q_ref, o_ref, qhi, qlo):
    @pl.when(pl.program_id(0) == 0)
    def _():
        for p in range(2):
            put_rotation([q_ref[p, i] for i in range(3)], qhi, qlo, p)

    for p in range(2):
        xh, xl = split(x_ref[:, 2 * p * BLK : (2 * p + 2) * BLK])
        for h in range(2):
            cols = slice(h * BLK, (h + 1) * BLK)
            o_ref[:, (2 * p + h) * BLK : (2 * p + h + 1) * BLK] = mm3(
                (xh, xl), (qhi[p, :, cols], qlo[p, :, cols])
            )


def last_rotation(x, q):
    rows = x.shape[0]
    step_rows = rows // 4
    return pl.pallas_call(
        rotate_kernel,
        grid=(rows // step_rows,),
        out_shape=jax.ShapeDtypeStruct(x.shape, f32),
        in_specs=[
            pl.BlockSpec((step_rows, 4 * BLK), lambda i: (i, 0)),
            pl.BlockSpec((2, 3, BLK, BLK), lambda i: (0, 0, 0, 0)),
        ],
        out_specs=pl.BlockSpec((step_rows, 4 * BLK), lambda i: (i, 0)),
        scratch_shapes=[pltpu.VMEM((2, 2 * BLK, 2 * BLK), bf16)] * 2,
        compiler_params=pltpu.CompilerParams(vmem_limit_bytes=60 << 20),
    )(x, q)


def shards(n_row, n_col, activations, plan):
    x2, q = two_rounds(plan, activations, n_row, n_col)
    return last_rotation(x2, q)


def solution(mesh):
    placed = (P("row", "col"), P())
    return jax.shard_map(
        functools.partial(shards, mesh.shape["row"], mesh.shape["col"]),
        mesh=mesh, in_specs=placed, out_specs=P("row", "col"), check_vma=False,
    )
```

```python
import functools
import math

import jax
import jax.numpy as jnp
from jax import lax
from jax.experimental import pallas as pl
from jax.experimental.pallas import tpu as pltpu
from jax.sharding import PartitionSpec as P

BLK = 256
HALF = 128
EPS = 1e-6
STEPS = 7
BOUND = 1.02 * (1.0 + (BLK / 2) ** 2 / 4)
MESH = pl.DeviceIdType.MESH
HIGHEST = lax.Precision.HIGHEST
f32, bf16 = jnp.float32, jnp.bfloat16


def split(value):
    hi = value.astype(bf16)
    return hi, (value - hi.astype(f32)).astype(bf16)


def mm(a, b):
    return lax.dot_general(a, b, (((1,), (0,)), ((), ())), preferred_element_type=f32)


def mm_t(a, b):
    return lax.dot_general(a, b, (((0,), (0,)), ((), ())), preferred_element_type=f32)


def mm3(a, b):
    return mm(a[0], b[0]) + (mm(a[0], b[1]) + mm(a[1], b[0]))


def full(a, b, dims):
    return lax.dot_general(a, b, (dims, ((), ())), precision=HIGHEST, preferred_element_type=f32)


def eye():
    rows = lax.broadcasted_iota(jnp.int32, (BLK, BLK), 0)
    cols = lax.broadcasted_iota(jnp.int32, (BLK, BLK), 1)
    return jnp.where(rows == cols, 1.0, 0.0).astype(f32)


def put_rotation(q, hi_ref, lo_ref, pair, whole_ref=None):
    q11, w, q22 = q
    for value, r, c in ((q11, 0, 0), (w, 0, 1), (-w.T, 1, 0), (q22, 1, 1)):
        hi, lo = split(value)
        hi_ref[pair, r * BLK : (r + 1) * BLK, c * BLK : (c + 1) * BLK] = hi
        lo_ref[pair, r * BLK : (r + 1) * BLK, c * BLK : (c + 1) * BLK] = lo
        if whole_ref is not None:
            whole_ref[2 * pair + c, r] = value


def rounds_kernel(
    n_row, n_col, rows,
    plan_ref, x_ref, x2_ref, q_ref,
    xv, nv, zsend, zrecv, gram, sq, part_send, part_recv, rs_src, rs_recv, ag, gmat, cmat, qv, qhi, qlo, qf,
    esend, erecv, zearly, qz, qz_all, qz_other,
    load_sem, part_s, part_r, rs_s, rs_r, ag_s, ag_r, q_s, q_r, z_s, z_r, out_sem,
    e_s, e_r, qz_s, qz_r, qa_s, qa_r, qp_s, qp_r,
):
    chips = n_row // 2
    crow = BLK // chips
    row, z = lax.axis_index("row"), lax.axis_index("col")
    core, chip = lax.rem(row, 2), row // 2
    other = 1 - core
    partner = (chip * 2 + other, z)
    z_up, z_down = lax.rem(z + 1, n_col), lax.rem(z + n_col - 1, n_col)
    unit = rows // 8
    late = [(0, 2 * unit), (2 * unit, 2 * unit), (4 * unit, unit)]
    early, n_early = 5 * unit, 3 * unit

    side = math.isqrt(chips)
    cx, cy = chip // side, lax.rem(chip, side)

    def hops(offset):
        return min(offset, side - offset)

    far_first = sorted(
        [(dx, dy) for dx in range(side) for dy in range(side) if (dx, dy) != (0, 0)],
        key=lambda d: -hops(d[0]) - hops(d[1]),
    )
    peers = []
    for dx, dy in far_first:
        t = lax.rem(cx + dx, side) * side + lax.rem(cy + dy, side)
        peers.append((t, (t * 2 + core, z)))

    loads = []
    for i, p in enumerate((other, core)):
        for h in range(2):
            cols = pl.ds(pl.multiple_of((2 * p + h) * BLK, BLK), BLK)
            loads.append(pltpu.make_async_copy(x_ref.at[:, cols], xv.at[2 * p + h], load_sem.at[2 * i + h]))
            loads[-1].start()

    barrier = pltpu.get_barrier_semaphore()

    for dev in [dev for _, dev in peers] + [(row, z_up), (row, z_down), partner]:
        pl.semaphore_signal(barrier, inc=1, device_id=dev, device_id_type=MESH)

    def gram_step(p, start, step_rows):
        rs = pl.ds(start, step_rows)
        lead, mate = xv[2 * p, rs, :], xv[2 * p + 1, rs, :]
        lh, ll = split(lead)
        mh, ml = split(mate)
        gram[p] += mm_t(lh, mh) + (mm_t(lh, ml) + mm_t(ll, mh))
        sq[p, 0] += jnp.sum((lead * lead).reshape(step_rows // 8, 8, BLK), axis=0)
        sq[p, 1] += jnp.sum((mate * mate).reshape(step_rows // 8, 8, BLK), axis=0)

    def squares(p):
        lead_sq = jnp.sum(sq[p, 0], axis=0, keepdims=True)
        mate_sq = jnp.sum(sq[p, 1], axis=0, keepdims=True)
        return jnp.concatenate(
            [lead_sq[:, :HALF], lead_sq[:, HALF:], mate_sq[:, :HALF], mate_sq[:, HALF:], jnp.zeros((4, HALF), f32)],
            axis=0,
        )

    def part_copy(rnd):
        return pltpu.make_async_remote_copy(
            part_send.at[rnd], part_recv.at[rnd], part_s.at[rnd], part_r.at[rnd], device_id=partner, device_id_type=MESH
        )

    def send_part(rnd):
        part_send[rnd, 0:BLK, :] = gram[other, :, 0:HALF]
        part_send[rnd, BLK : 2 * BLK, :] = gram[other, :, HALF:BLK]
        part_send[rnd, 2 * BLK : 2 * BLK + 8, :] = squares(other)
        part_copy(rnd).start()

    def reduce_gram(rnd):
        own_sq = squares(core)
        part_copy(rnd).wait()
        left = gram[core, :, 0:HALF] + part_recv[rnd, 0:BLK, :]
        right = gram[core, :, HALF:BLK] + part_recv[rnd, BLK : 2 * BLK, :]
        both_sq = own_sq + part_recv[rnd, 2 * BLK : 2 * BLK + 8, :]
        rs_src[rnd, :, 0:crow, :] = left.reshape(chips, crow, HALF)
        rs_src[rnd, :, crow : 2 * crow, :] = right.reshape(chips, crow, HALF)
        rs_src[rnd, :, 2 * crow : 2 * crow + 8, :] = jnp.broadcast_to(both_sq[None], (chips, 8, HALF))

        sent = crow * 2 + 4

        def rs_copy(k, t, dev, source):
            return pltpu.make_async_remote_copy(
                rs_src.at[rnd, t, 0:sent], rs_recv.at[rnd, source, 0:sent], rs_s.at[rnd, k], rs_r.at[rnd, source],
                device_id=dev, device_id_type=MESH,
            )

        def ag_copy(k, dev, source):
            return pltpu.make_async_remote_copy(
                ag.at[rnd, source], ag.at[rnd, source], ag_s.at[rnd, k], ag_r.at[rnd, source],
                device_id=dev, device_id_type=MESH,
            )

        for k, (t, dev) in enumerate(peers):
            rs_copy(k, t, dev, chip).start()
        rs_recv[rnd, chip] = rs_src[rnd, chip]
        for k, (t, dev) in enumerate(peers):
            rs_copy(k, t, dev, t).wait_recv()
        total = jnp.sum(rs_recv[rnd], axis=0)
        ag[rnd, chip] = total[0 : 2 * crow]
        for k, (t, dev) in enumerate(peers):
            ag_copy(k, dev, chip).start()
        for k, (t, dev) in enumerate(peers):
            rs_copy(k, t, dev, chip).wait_send()
        for k, (t, dev) in enumerate(peers):
            ag_copy(k, dev, t).wait_recv()
        for k, (t, dev) in enumerate(peers):
            ag_copy(k, dev, chip).wait_send()
        return total[2 * crow : 2 * crow + 8]

    def rotation(rnd, sums):
        lead_sq = jnp.concatenate([sums[0:1], sums[1:2]], axis=1)
        mate_sq = jnp.concatenate([sums[2:3], sums[3:4]], axis=1)
        lead_col = jnp.broadcast_to(lead_sq, (8, BLK)).T[:, 0:1]
        cross = jnp.concatenate(
            [ag[rnd, :, 0:crow, :].reshape(BLK, HALF), ag[rnd, :, crow : 2 * crow, :].reshape(BLK, HALF)], axis=1
        )
        cmat[...] = cross / (lead_col + mate_sq + EPS)
        ident = eye()
        gmat[...] = ident + 0.25 * full(cmat[...], cmat[...], ((1,), (1,)))
        scale = 2.0 / (1.0 + BOUND)
        radius = (BOUND - 1.0) / (BOUND + 1.0)
        res = split(ident - scale * gmat[...])
        inv = None
        for k in range(STEPS):
            s = 2.0 / (2.0 - radius * radius)
            radius = radius * radius / (2.0 - radius * radius)
            if k < STEPS - 1:
                square = mm3(res, res)
            if k == 0:
                inv = (s * scale) * (ident + (res[0].astype(f32) + res[1].astype(f32)))
            else:
                inv = s * (inv + mm3(split(inv), res))
            if k < STEPS - 1:
                res = split(s * square + (1.0 - s) * ident)
        inv_parts = split(inv)
        inv = inv + mm3(inv_parts, split(ident - mm3(split(gmat[...]), inv_parts)))
        inv = inv + mm3(split(inv), split(ident - full(gmat[...], inv, ((1,), (0,)))))
        w = full(inv, cmat[...], ((1,), (0,)))
        qv[rnd, core, 0] = 2.0 * inv - ident
        qv[rnd, core, 1] = w
        qv[rnd, core, 2] = ident - 0.5 * full(cmat[...], w, ((0,), (0,)))

    def q_copy(rnd, p):
        return pltpu.make_async_remote_copy(
            qv.at[rnd, p], qv.at[rnd, p], q_s.at[rnd], q_r.at[rnd], device_id=partner, device_id_type=MESH
        )

    def q_out(p):
        return pltpu.make_async_remote_copy(
            qv.at[1, p], q_ref.at[p], q_s.at[1], q_r.at[1], device_id=partner, device_id_type=MESH
        )

    def rotate(p, start, step_rows):
        rs = pl.ds(start, step_rows)
        x = jnp.concatenate([xv[2 * p, rs, :], xv[2 * p + 1, rs, :]], axis=1)
        xh, xl = split(x)
        for h in range(2):
            cols = slice(h * BLK, (h + 1) * BLK)
            nv[2 * p + h, rs, :] = mm3((xh, xl), (qhi[p, :, cols], qlo[p, :, cols]))

    up_slot = down_slot = jnp.int32(0)
    for j in range(4):
        above, below = plan_ref[1, z_up * 4 + j], plan_ref[1, z_down * 4 + j]
        up_slot = jnp.where(above // 4 == z, above - 4 * z, up_slot)
        down_slot = jnp.where(below // 4 == z, below - 4 * z, down_slot)
    origin = [plan_ref[1, z * 4 + j] for j in range(4)]

    def z_copy(way, i):
        rs = pl.ds(*late[i])
        return pltpu.make_async_remote_copy(
            zsend.at[way, rs, :], zrecv.at[way, rs, :], z_s.at[way, i], z_r.at[way, i],
            device_id=(row, z_up if way == 0 else z_down), device_id_type=MESH,
        )

    def early_copy(way):
        return pltpu.make_async_remote_copy(
            esend.at[way], erecv.at[way], e_s.at[way], e_r.at[way],
            device_id=(row, z_up if way == 0 else z_down), device_id_type=MESH,
        )

    def share_copy(way):
        return pltpu.make_async_remote_copy(
            qz.at[way], qz_all.at[chip, way], qz_s.at[way], qz_r.at[way],
            device_id=(row, z_up if way == 0 else z_down), device_id_type=MESH,
        )

    def share_gather(k, dev, source):
        return pltpu.make_async_remote_copy(
            qz_all.at[source], qz_all.at[source], qa_s.at[k], qa_r.at[source], device_id=dev, device_id_type=MESH
        )

    def share_swap():
        return pltpu.make_async_remote_copy(
            qz_all, qz_other, qp_s.at[0], qp_r.at[0], device_id=partner, device_id_type=MESH
        )

    gram[...] = jnp.zeros_like(gram)
    sq[...] = jnp.zeros_like(sq)
    loads[0].wait()
    loads[1].wait()
    for start in range(0, rows, 2 * unit):
        gram_step(other, start, 2 * unit)
    loads[2].wait()
    loads[3].wait()
    pl.semaphore_wait(barrier, chips + 2)
    send_part(0)
    for way, slot in enumerate((up_slot, down_slot)):
        for h in range(2):
            esend[way, h] = xv[(slot // 2) * 2 + h, pl.ds(early, n_early), :]
        early_copy(way).start()
    for start in range(0, rows, 2 * unit):
        gram_step(core, start, 2 * unit)
    rotation(0, reduce_gram(0))
    q_copy(0, core).start()
    put_rotation([qv[0, core, i] for i in range(3)], qhi, qlo, core, qf)
    for start, size in late:
        rotate(core, start, size)
    q_copy(0, core).wait_send()
    q_copy(0, other).wait_recv()
    put_rotation([qv[0, other, i] for i in range(3)], qhi, qlo, other, qf)
    for way, slot in enumerate((up_slot, down_slot)):
        qz[way] = qf[slot, core, pl.ds(pl.multiple_of(chip * crow, crow), crow), :]
        share_copy(way).start()
    for i, (start, size) in enumerate(late):
        rotate(other, start, size)
        rs = pl.ds(start, size)
        zsend[0, rs, :] = nv[up_slot, rs, :]
        z_copy(0, i).start()
        zsend[1, rs, :] = nv[down_slot, rs, :]
        z_copy(1, i).start()
    for way in range(2):
        share_copy(way).wait_recv()
    for k, (_, dev) in enumerate(peers):
        share_gather(k, dev, chip).start()
    rotate(core, early, n_early)
    rotate(other, early, n_early)

    gram[...] = jnp.zeros_like(gram)
    sq[...] = jnp.zeros_like(sq)
    outs = []

    def place(start, size, lower, upper):
        rs = pl.ds(start, size)
        for j in range(4):
            home = origin[j] // 4
            own = nv[jnp.clip(origin[j] - 4 * z, 0, 3), rs, :]
            xv[j, rs, :] = jnp.where(home == z, own, jnp.where(home < z, lower[...], upper[...]))
            outs.append(
                pltpu.make_async_copy(
                    xv.at[j, rs, :], x2_ref.at[rs, j * BLK : (j + 1) * BLK], out_sem.at[len(outs)]
                )
            )
            outs[-1].start()

    def arrive(i):
        z_copy(0, i).wait_recv()
        z_copy(1, i).wait_recv()
        rs = pl.ds(*late[i])
        place(*late[i], zrecv.at[0, rs, :], zrecv.at[1, rs, :])

    arrive(0)
    gram_step(other, *late[0])
    gram_step(core, *late[0])
    for k, (t, dev) in enumerate(peers):
        share_gather(k, dev, t).wait_recv()
    share_swap().start()
    for way in range(2):
        early_copy(way).wait_recv()
    for way in range(2):
        part = qz_all[:, way].reshape(BLK, BLK)
        zearly[way] = mm3(split(erecv[way, core]), split(part))
    share_swap().wait_recv()
    for way in range(2):
        part = qz_other[:, way].reshape(BLK, BLK)
        zearly[way] += mm3(split(erecv[way, other]), split(part))
    place(early, n_early, zearly.at[0], zearly.at[1])
    gram_step(other, early, n_early)
    gram_step(core, early, n_early)
    arrive(1)
    gram_step(other, *late[1])
    gram_step(core, *late[1])
    arrive(2)
    gram_step(other, *late[2])
    send_part(1)
    gram_step(core, *late[2])
    for way in range(2):
        for i in range(len(late)):
            z_copy(way, i).wait_send()
        early_copy(way).wait_send()
        share_copy(way).wait_send()
    for k, (_, dev) in enumerate(peers):
        share_gather(k, dev, chip).wait_send()
    share_swap().wait_send()
    rotation(1, reduce_gram(1))
    q_out(core).start()
    final = pltpu.make_async_copy(qv.at[1, core], q_ref.at[core], load_sem.at[0])
    final.start()
    for copy in outs:
        copy.wait()
    final.wait()
    q_out(core).wait_send()
    q_out(other).wait_recv()


def two_rounds(plan, x, n_row, n_col):
    rows = x.shape[0]
    n_early = 3 * rows // 8
    chips = n_row // 2
    crow = BLK // chips
    dma = pltpu.SemaphoreType.DMA
    return pl.pallas_call(
        functools.partial(rounds_kernel, n_row, n_col, rows),
        out_shape=[jax.ShapeDtypeStruct(x.shape, f32), jax.ShapeDtypeStruct((2, 3, BLK, BLK), f32)],
        in_specs=[pl.BlockSpec(memory_space=pltpu.SMEM), pl.BlockSpec(memory_space=pl.ANY)],
        out_specs=[pl.BlockSpec(memory_space=pl.ANY)] * 2,
        scratch_shapes=[
            pltpu.VMEM((4, rows, BLK), f32),
            pltpu.VMEM((4, rows, BLK), f32),
            pltpu.VMEM((2, rows, BLK), f32),
            pltpu.VMEM((2, rows, BLK), f32),
            pltpu.VMEM((2, BLK, BLK), f32),
            pltpu.VMEM((2, 2, 8, BLK), f32),
            pltpu.VMEM((2, 2 * BLK + 8, HALF), f32),
            pltpu.VMEM((2, 2 * BLK + 8, HALF), f32),
            pltpu.VMEM((2, chips, 2 * crow + 8, HALF), f32),
            pltpu.VMEM((2, chips, 2 * crow + 8, HALF), f32),
            pltpu.VMEM((2, chips, 2 * crow, HALF), f32),
            pltpu.VMEM((BLK, BLK), f32),
            pltpu.VMEM((BLK, BLK), f32),
            pltpu.VMEM((2, 2, 3, BLK, BLK), f32),
            pltpu.VMEM((2, 2 * BLK, 2 * BLK), bf16),
            pltpu.VMEM((2, 2 * BLK, 2 * BLK), bf16),
            pltpu.VMEM((4, 2, BLK, BLK), f32),
            pltpu.VMEM((2, 2, n_early, BLK), f32),
            pltpu.VMEM((2, 2, n_early, BLK), f32),
            pltpu.VMEM((2, n_early, BLK), f32),
            pltpu.VMEM((2, crow, BLK), f32),
            pltpu.VMEM((chips, 2, crow, BLK), f32),
            pltpu.VMEM((chips, 2, crow, BLK), f32),
            dma((4,)),
            dma((2,)), dma((2,)),
            dma((2, chips)), dma((2, chips)),
            dma((2, chips)), dma((2, chips)),
            dma((2,)), dma((2,)),
            dma((2, 3)), dma((2, 3)),
            dma((16,)),
            dma((2,)), dma((2,)),
            dma((2,)), dma((2,)),
            dma((chips,)), dma((chips,)),
            dma((1,)), dma((1,)),
        ],
        compiler_params=pltpu.CompilerParams(collective_id=0, has_side_effects=True, vmem_limit_bytes=48 << 20),
    )(plan, x)


def rotate_kernel(step_rows, x_ref, q_ref, o_ref, qhi, qlo):
    @pl.when(pl.program_id(0) == 0)
    def _():
        for p in range(2):
            put_rotation([q_ref[p, i] for i in range(3)], qhi, qlo, p)

    rs = pl.ds(pl.multiple_of(pl.program_id(0) * step_rows, step_rows), step_rows)
    for p in range(2):
        xh, xl = split(x_ref[rs, 2 * p * BLK : (2 * p + 2) * BLK])
        for h in range(2):
            cols = slice(h * BLK, (h + 1) * BLK)
            o_ref[:, (2 * p + h) * BLK : (2 * p + h + 1) * BLK] = mm3(
                (xh, xl), (qhi[p, :, cols], qlo[p, :, cols])
            )


def last_rotation(x, q):
    rows = x.shape[0]
    step_rows = rows // 4
    return pl.pallas_call(
        functools.partial(rotate_kernel, step_rows),
        grid=(rows // step_rows,),
        out_shape=jax.ShapeDtypeStruct(x.shape, f32),
        in_specs=[pl.BlockSpec(memory_space=pltpu.VMEM)] * 2,
        out_specs=pl.BlockSpec((step_rows, 4 * BLK), lambda i: (i, 0)),
        scratch_shapes=[pltpu.VMEM((2, 2 * BLK, 2 * BLK), bf16)] * 2,
        compiler_params=pltpu.CompilerParams(vmem_limit_bytes=20 << 20),
    )(x, q)


def shards(n_row, n_col, activations, plan):
    x2, q = two_rounds(plan, activations, n_row, n_col)
    return last_rotation(x2, q)


def solution(mesh):
    placed = (P("row", "col"), P())
    return jax.shard_map(
        functools.partial(shards, mesh.shape["row"], mesh.shape["col"]),
        mesh=mesh, in_specs=placed, out_specs=P("row", "col"), check_vma=False,
    )
```

```python
import functools
import math

import jax
import jax.numpy as jnp
from jax import lax
from jax.experimental import pallas as pl
from jax.experimental.pallas import tpu as pltpu
from jax.sharding import PartitionSpec as P

BLK = 256
HALF = 128
EPS = 1e-6
STEPS = 7
BOUND = 1.02 * (1.0 + (BLK / 2) ** 2 / 4)
MESH = pl.DeviceIdType.MESH
HIGHEST = lax.Precision.HIGHEST
f32, bf16 = jnp.float32, jnp.bfloat16


def split(value):
    hi = value.astype(bf16)
    return hi, (value - hi.astype(f32)).astype(bf16)


def mm(a, b):
    return lax.dot_general(a, b, (((1,), (0,)), ((), ())), preferred_element_type=f32)


def mm_t(a, b):
    return lax.dot_general(a, b, (((0,), (0,)), ((), ())), preferred_element_type=f32)


def mm3(a, b):
    return mm(a[0], b[0]) + (mm(a[0], b[1]) + mm(a[1], b[0]))


def full(a, b, dims):
    return lax.dot_general(a, b, (dims, ((), ())), precision=HIGHEST, preferred_element_type=f32)


def eye():
    rows = lax.broadcasted_iota(jnp.int32, (BLK, BLK), 0)
    cols = lax.broadcasted_iota(jnp.int32, (BLK, BLK), 1)
    return jnp.where(rows == cols, 1.0, 0.0).astype(f32)


def put_rotation(q, hi_ref, lo_ref, pair, whole_ref=None):
    q11, w, q22 = q
    for value, r, c in ((q11, 0, 0), (w, 0, 1), (-w.T, 1, 0), (q22, 1, 1)):
        hi, lo = split(value)
        hi_ref[pair, r * BLK : (r + 1) * BLK, c * BLK : (c + 1) * BLK] = hi
        lo_ref[pair, r * BLK : (r + 1) * BLK, c * BLK : (c + 1) * BLK] = lo
        if whole_ref is not None:
            whole_ref[2 * pair + c, r] = value


def rounds_kernel(
    n_row, n_col, rows,
    plan_ref, x_ref, xh_ref, xl_ref, qh_ref, ql_ref,
    xv, nv, zsend, zrecv, gram, sq, part_send, part_recv, rs_src, rs_recv, ag, gmat, cmat, qv, qhi, qlo, qf,
    esend, erecv, zearly, qz, qz_all, qz_other,
    load_sem, part_s, part_r, rs_s, rs_r, ag_s, ag_r, q_s, q_r, z_s, z_r,
    e_s, e_r, qz_s, qz_r, qa_s, qa_r, qp_s, qp_r,
):
    chips = n_row // 2
    crow = BLK // chips
    row, z = lax.axis_index("row"), lax.axis_index("col")
    core, chip = lax.rem(row, 2), row // 2
    other = 1 - core
    partner = (chip * 2 + other, z)
    z_up, z_down = lax.rem(z + 1, n_col), lax.rem(z + n_col - 1, n_col)
    unit = rows // 8
    late = [(0, 2 * unit), (2 * unit, unit), (3 * unit, unit)]
    early, n_early = 4 * unit, 4 * unit

    side = math.isqrt(chips)
    cx, cy = chip // side, lax.rem(chip, side)

    def hops(offset):
        return min(offset, side - offset)

    far_first = sorted(
        [(dx, dy) for dx in range(side) for dy in range(side) if (dx, dy) != (0, 0)],
        key=lambda d: -hops(d[0]) - hops(d[1]),
    )
    peers = []
    for dx, dy in far_first:
        t = lax.rem(cx + dx, side) * side + lax.rem(cy + dy, side)
        peers.append((t, (t * 2 + core, z)))

    loads = []
    for i, p in enumerate((other, core)):
        for h in range(2):
            cols = pl.ds(pl.multiple_of((2 * p + h) * BLK, BLK), BLK)
            loads.append(pltpu.make_async_copy(x_ref.at[:, cols], xv.at[2 * p + h], load_sem.at[2 * i + h]))
            loads[-1].start()

    barrier = pltpu.get_barrier_semaphore()

    for dev in [dev for _, dev in peers] + [(row, z_up), (row, z_down), partner]:
        pl.semaphore_signal(barrier, inc=1, device_id=dev, device_id_type=MESH)

    def gram_step(p, start, step_rows, keep=False):
        rs = pl.ds(start, step_rows)
        lead, mate = xv[2 * p, rs, :], xv[2 * p + 1, rs, :]
        lh, ll = split(lead)
        mh, ml = split(mate)
        if keep:
            for h, hi, lo in ((0, lh, ll), (1, mh, ml)):
                cols = pl.ds(pl.multiple_of((2 * p + h) * BLK, BLK), BLK)
                xh_ref[rs, cols] = hi
                xl_ref[rs, cols] = lo
        gram[p] += mm_t(lh, mh) + (mm_t(lh, ml) + mm_t(ll, mh))
        sq[p, 0] += jnp.sum((lead * lead).reshape(step_rows // 8, 8, BLK), axis=0)
        sq[p, 1] += jnp.sum((mate * mate).reshape(step_rows // 8, 8, BLK), axis=0)

    def squares(p):
        lead_sq = jnp.sum(sq[p, 0], axis=0, keepdims=True)
        mate_sq = jnp.sum(sq[p, 1], axis=0, keepdims=True)
        return jnp.concatenate(
            [lead_sq[:, :HALF], lead_sq[:, HALF:], mate_sq[:, :HALF], mate_sq[:, HALF:], jnp.zeros((4, HALF), f32)],
            axis=0,
        )

    def part_copy(rnd):
        return pltpu.make_async_remote_copy(
            part_send.at[rnd], part_recv.at[rnd], part_s.at[rnd], part_r.at[rnd], device_id=partner, device_id_type=MESH
        )

    def send_part(rnd):
        part_send[rnd, 0:BLK, :] = gram[other, :, 0:HALF]
        part_send[rnd, BLK : 2 * BLK, :] = gram[other, :, HALF:BLK]
        part_send[rnd, 2 * BLK : 2 * BLK + 8, :] = squares(other)
        part_copy(rnd).start()

    def reduce_gram(rnd):
        own_sq = squares(core)
        part_copy(rnd).wait()
        left = gram[core, :, 0:HALF] + part_recv[rnd, 0:BLK, :]
        right = gram[core, :, HALF:BLK] + part_recv[rnd, BLK : 2 * BLK, :]
        both_sq = own_sq + part_recv[rnd, 2 * BLK : 2 * BLK + 8, :]
        rs_src[rnd, :, 0:crow, :] = left.reshape(chips, crow, HALF)
        rs_src[rnd, :, crow : 2 * crow, :] = right.reshape(chips, crow, HALF)
        rs_src[rnd, :, 2 * crow : 2 * crow + 8, :] = jnp.broadcast_to(both_sq[None], (chips, 8, HALF))

        sent = crow * 2 + 4

        def rs_copy(k, t, dev, source):
            return pltpu.make_async_remote_copy(
                rs_src.at[rnd, t, 0:sent], rs_recv.at[rnd, source, 0:sent], rs_s.at[rnd, k], rs_r.at[rnd, source],
                device_id=dev, device_id_type=MESH,
            )

        def ag_copy(k, dev, source):
            return pltpu.make_async_remote_copy(
                ag.at[rnd, source], ag.at[rnd, source], ag_s.at[rnd, k], ag_r.at[rnd, source],
                device_id=dev, device_id_type=MESH,
            )

        for k, (t, dev) in enumerate(peers):
            rs_copy(k, t, dev, chip).start()
        rs_recv[rnd, chip] = rs_src[rnd, chip]
        for k, (t, dev) in enumerate(peers):
            rs_copy(k, t, dev, t).wait_recv()
        total = jnp.sum(rs_recv[rnd], axis=0)
        ag[rnd, chip] = total[0 : 2 * crow]
        for k, (t, dev) in enumerate(peers):
            ag_copy(k, dev, chip).start()
        for k, (t, dev) in enumerate(peers):
            rs_copy(k, t, dev, chip).wait_send()
        for k, (t, dev) in enumerate(peers):
            ag_copy(k, dev, t).wait_recv()
        for k, (t, dev) in enumerate(peers):
            ag_copy(k, dev, chip).wait_send()
        return total[2 * crow : 2 * crow + 8]

    def rotation(rnd, sums):
        lead_sq = jnp.concatenate([sums[0:1], sums[1:2]], axis=1)
        mate_sq = jnp.concatenate([sums[2:3], sums[3:4]], axis=1)
        lead_col = jnp.broadcast_to(lead_sq, (8, BLK)).T[:, 0:1]
        cross = jnp.concatenate(
            [ag[rnd, :, 0:crow, :].reshape(BLK, HALF), ag[rnd, :, crow : 2 * crow, :].reshape(BLK, HALF)], axis=1
        )
        cmat[...] = cross / (lead_col + mate_sq + EPS)
        ident = eye()
        gmat[...] = ident + 0.25 * full(cmat[...], cmat[...], ((1,), (1,)))
        scale = 2.0 / (1.0 + BOUND)
        radius = (BOUND - 1.0) / (BOUND + 1.0)
        res = split(ident - scale * gmat[...])
        inv = None
        for k in range(STEPS):
            s = 2.0 / (2.0 - radius * radius)
            radius = radius * radius / (2.0 - radius * radius)
            if k < STEPS - 1:
                square = mm3(res, res)
            if k == 0:
                inv = (s * scale) * (ident + (res[0].astype(f32) + res[1].astype(f32)))
            else:
                inv = s * (inv + mm3(split(inv), res))
            if k < STEPS - 1:
                res = split(s * square + (1.0 - s) * ident)
        inv_parts = split(inv)
        inv = inv + mm3(inv_parts, split(ident - mm3(split(gmat[...]), inv_parts)))
        inv = inv + mm3(split(inv), split(ident - full(gmat[...], inv, ((1,), (0,)))))
        w = full(inv, cmat[...], ((1,), (0,)))
        qv[rnd, core, 0] = 2.0 * inv - ident
        qv[rnd, core, 1] = w
        qv[rnd, core, 2] = ident - 0.5 * full(cmat[...], w, ((0,), (0,)))

    def q_copy(rnd, p):
        return pltpu.make_async_remote_copy(
            qv.at[rnd, p], qv.at[rnd, p], q_s.at[rnd], q_r.at[rnd], device_id=partner, device_id_type=MESH
        )

    def rotate(p, start, step_rows):
        rs = pl.ds(start, step_rows)
        x = jnp.concatenate([xv[2 * p, rs, :], xv[2 * p + 1, rs, :]], axis=1)
        xh, xl = split(x)
        for h in range(2):
            cols = slice(h * BLK, (h + 1) * BLK)
            nv[2 * p + h, rs, :] = mm3((xh, xl), (qhi[p, :, cols], qlo[p, :, cols]))

    up_slot = down_slot = jnp.int32(0)
    for j in range(4):
        above, below = plan_ref[1, z_up * 4 + j], plan_ref[1, z_down * 4 + j]
        up_slot = jnp.where(above // 4 == z, above - 4 * z, up_slot)
        down_slot = jnp.where(below // 4 == z, below - 4 * z, down_slot)
    origin = [plan_ref[1, z * 4 + j] for j in range(4)]

    def z_copy(way, i):
        rs = pl.ds(*late[i])
        return pltpu.make_async_remote_copy(
            zsend.at[way, rs, :], zrecv.at[way, rs, :], z_s.at[way, i], z_r.at[way, i],
            device_id=(row, z_up if way == 0 else z_down), device_id_type=MESH,
        )

    def early_copy(way):
        return pltpu.make_async_remote_copy(
            esend.at[way], erecv.at[way], e_s.at[way], e_r.at[way],
            device_id=(row, z_up if way == 0 else z_down), device_id_type=MESH,
        )

    def share_copy(way):
        return pltpu.make_async_remote_copy(
            qz.at[way], qz_all.at[chip, way], qz_s.at[way], qz_r.at[way],
            device_id=(row, z_up if way == 0 else z_down), device_id_type=MESH,
        )

    def share_gather(k, dev, source):
        return pltpu.make_async_remote_copy(
            qz_all.at[source], qz_all.at[source], qa_s.at[k], qa_r.at[source], device_id=dev, device_id_type=MESH
        )

    def share_swap():
        return pltpu.make_async_remote_copy(
            qz_all, qz_other, qp_s.at[0], qp_r.at[0], device_id=partner, device_id_type=MESH
        )

    gram[...] = jnp.zeros_like(gram)
    sq[...] = jnp.zeros_like(sq)
    loads[0].wait()
    loads[1].wait()
    for start in range(0, rows, 2 * unit):
        gram_step(other, start, 2 * unit)
    loads[2].wait()
    loads[3].wait()
    for way, slot in enumerate((up_slot, down_slot)):
        for h in range(2):
            esend[way, h] = xv[(slot // 2) * 2 + h, pl.ds(early, n_early), :]
    pl.semaphore_wait(barrier, chips + 2)
    for way in range(2):
        early_copy(way).start()
    send_part(0)
    for start in range(0, rows, 2 * unit):
        gram_step(core, start, 2 * unit)
    rotation(0, reduce_gram(0))
    q_copy(0, core).start()
    put_rotation([qv[0, core, i] for i in range(3)], qhi, qlo, core, qf)
    for start, size in late:
        rotate(core, start, size)
    q_copy(0, core).wait_send()
    q_copy(0, other).wait_recv()
    put_rotation([qv[0, other, i] for i in range(3)], qhi, qlo, other, qf)
    for way, slot in enumerate((up_slot, down_slot)):
        qz[way] = qf[slot, core, pl.ds(pl.multiple_of(chip * crow, crow), crow), :]
        share_copy(way).start()
    for i, (start, size) in enumerate(late):
        rotate(other, start, size)
        rs = pl.ds(start, size)
        zsend[0, rs, :] = nv[up_slot, rs, :]
        z_copy(0, i).start()
        zsend[1, rs, :] = nv[down_slot, rs, :]
        z_copy(1, i).start()
    for way in range(2):
        share_copy(way).wait_recv()
    for k, (_, dev) in enumerate(peers):
        share_gather(k, dev, chip).start()
    rotate(core, early, n_early)
    rotate(other, early, n_early)

    gram[...] = jnp.zeros_like(gram)
    sq[...] = jnp.zeros_like(sq)

    def place(start, size, lower, upper):
        rs = pl.ds(start, size)
        for j in range(4):
            home = origin[j] // 4
            own = nv[jnp.clip(origin[j] - 4 * z, 0, 3), rs, :]
            xv[j, rs, :] = jnp.where(home == z, own, jnp.where(home < z, lower[...], upper[...]))

    def arrive(i):
        z_copy(0, i).wait_recv()
        z_copy(1, i).wait_recv()
        rs = pl.ds(*late[i])
        place(*late[i], zrecv.at[0, rs, :], zrecv.at[1, rs, :])

    arrive(0)
    gram_step(other, *late[0], True)
    gram_step(core, *late[0], True)
    for k, (t, dev) in enumerate(peers):
        share_gather(k, dev, t).wait_recv()
    share_swap().start()
    for way in range(2):
        early_copy(way).wait_recv()
    for way in range(2):
        part = qz_all[:, way].reshape(BLK, BLK)
        zearly[way] = mm3(split(erecv[way, core]), split(part))
    share_swap().wait_recv()
    for way in range(2):
        part = qz_other[:, way].reshape(BLK, BLK)
        zearly[way] += mm3(split(erecv[way, other]), split(part))
    place(early, n_early, zearly.at[0], zearly.at[1])
    gram_step(other, early, n_early, True)
    gram_step(core, early, n_early, True)
    arrive(1)
    gram_step(other, *late[1], True)
    gram_step(core, *late[1], True)
    arrive(2)
    gram_step(other, *late[2], True)
    send_part(1)
    gram_step(core, *late[2], True)
    for way in range(2):
        for i in range(len(late)):
            z_copy(way, i).wait_send()
        early_copy(way).wait_send()
        share_copy(way).wait_send()
    for k, (_, dev) in enumerate(peers):
        share_gather(k, dev, chip).wait_send()
    share_swap().wait_send()
    rotation(1, reduce_gram(1))
    q_copy(1, core).start()
    put_rotation([qv[1, core, i] for i in range(3)], qh_ref, ql_ref, core)
    q_copy(1, core).wait_send()
    q_copy(1, other).wait_recv()
    put_rotation([qv[1, other, i] for i in range(3)], qh_ref, ql_ref, other)


def two_rounds(plan, x, n_row, n_col):
    rows = x.shape[0]
    n_early = rows // 2
    chips = n_row // 2
    crow = BLK // chips
    dma = pltpu.SemaphoreType.DMA
    return pl.pallas_call(
        functools.partial(rounds_kernel, n_row, n_col, rows),
        out_shape=[jax.ShapeDtypeStruct(x.shape, bf16)] * 2 + [jax.ShapeDtypeStruct((2, 2 * BLK, 2 * BLK), bf16)] * 2,
        in_specs=[pl.BlockSpec(memory_space=pltpu.SMEM), pl.BlockSpec(memory_space=pl.ANY)],
        out_specs=[pl.BlockSpec(memory_space=pltpu.VMEM)] * 4,
        scratch_shapes=[
            pltpu.VMEM((4, rows, BLK), f32),
            pltpu.VMEM((4, rows, BLK), f32),
            pltpu.VMEM((2, rows, BLK), f32),
            pltpu.VMEM((2, rows, BLK), f32),
            pltpu.VMEM((2, BLK, BLK), f32),
            pltpu.VMEM((2, 2, 8, BLK), f32),
            pltpu.VMEM((2, 2 * BLK + 8, HALF), f32),
            pltpu.VMEM((2, 2 * BLK + 8, HALF), f32),
            pltpu.VMEM((2, chips, 2 * crow + 8, HALF), f32),
            pltpu.VMEM((2, chips, 2 * crow + 8, HALF), f32),
            pltpu.VMEM((2, chips, 2 * crow, HALF), f32),
            pltpu.VMEM((BLK, BLK), f32),
            pltpu.VMEM((BLK, BLK), f32),
            pltpu.VMEM((2, 2, 3, BLK, BLK), f32),
            pltpu.VMEM((2, 2 * BLK, 2 * BLK), bf16),
            pltpu.VMEM((2, 2 * BLK, 2 * BLK), bf16),
            pltpu.VMEM((4, 2, BLK, BLK), f32),
            pltpu.VMEM((2, 2, n_early, BLK), f32),
            pltpu.VMEM((2, 2, n_early, BLK), f32),
            pltpu.VMEM((2, n_early, BLK), f32),
            pltpu.VMEM((2, crow, BLK), f32),
            pltpu.VMEM((chips, 2, crow, BLK), f32),
            pltpu.VMEM((chips, 2, crow, BLK), f32),
            dma((4,)),
            dma((2,)), dma((2,)),
            dma((2, chips)), dma((2, chips)),
            dma((2, chips)), dma((2, chips)),
            dma((2,)), dma((2,)),
            dma((2, 3)), dma((2, 3)),
            dma((2,)), dma((2,)),
            dma((2,)), dma((2,)),
            dma((chips,)), dma((chips,)),
            dma((1,)), dma((1,)),
        ],
        compiler_params=pltpu.CompilerParams(collective_id=0, has_side_effects=True, vmem_limit_bytes=46 << 20),
    )(plan, x)


def rotate_kernel(step_rows, xh_ref, xl_ref, qh_ref, ql_ref, o_ref):
    rs = pl.ds(pl.multiple_of(pl.program_id(0) * step_rows, step_rows), step_rows)
    for p in range(2):
        pair = slice(2 * p * BLK, (2 * p + 2) * BLK)
        x = xh_ref[rs, pair], xl_ref[rs, pair]
        for h in range(2):
            cols = slice(h * BLK, (h + 1) * BLK)
            o_ref[:, (2 * p + h) * BLK : (2 * p + h + 1) * BLK] = mm3(x, (qh_ref[p, :, cols], ql_ref[p, :, cols]))


def last_rotation(xh, xl, qh, ql):
    rows = xh.shape[0]
    step_rows = rows // 4
    return pl.pallas_call(
        functools.partial(rotate_kernel, step_rows),
        grid=(rows // step_rows,),
        out_shape=jax.ShapeDtypeStruct(xh.shape, f32),
        in_specs=[pl.BlockSpec(memory_space=pltpu.VMEM)] * 4,
        out_specs=pl.BlockSpec((step_rows, 4 * BLK), lambda i: (i, 0)),
        compiler_params=pltpu.CompilerParams(vmem_limit_bytes=20 << 20),
    )(xh, xl, qh, ql)


def shards(n_row, n_col, activations, plan):
    return last_rotation(*two_rounds(plan, activations, n_row, n_col))


def solution(mesh):
    placed = (P("row", "col"), P())
    return jax.shard_map(
        functools.partial(shards, mesh.shape["row"], mesh.shape["col"]),
        mesh=mesh, in_specs=placed, out_specs=P("row", "col"), check_vma=False,
    )
```

```python
import functools
import math

import jax
import jax.numpy as jnp
from jax import lax
from jax.experimental import pallas as pl
from jax.experimental.pallas import tpu as pltpu
from jax.sharding import PartitionSpec as P

BLK = 256
HALF = 128
EPS = 1e-6
STEPS = 7
BOUND = 1.02 * (1.0 + (BLK / 2) ** 2 / 4)
MESH = pl.DeviceIdType.MESH
HIGHEST = lax.Precision.HIGHEST
f32, bf16 = jnp.float32, jnp.bfloat16


def split(value):
    hi = value.astype(bf16)
    return hi, (value - hi.astype(f32)).astype(bf16)


def mm(a, b):
    return lax.dot_general(a, b, (((1,), (0,)), ((), ())), preferred_element_type=f32)


def mm_t(a, b):
    return lax.dot_general(a, b, (((0,), (0,)), ((), ())), preferred_element_type=f32)


def mm3(a, b):
    return mm(a[0], b[0]) + (mm(a[0], b[1]) + mm(a[1], b[0]))


def full(a, b, dims):
    return lax.dot_general(a, b, (dims, ((), ())), precision=HIGHEST, preferred_element_type=f32)


def eye():
    rows = lax.broadcasted_iota(jnp.int32, (BLK, BLK), 0)
    cols = lax.broadcasted_iota(jnp.int32, (BLK, BLK), 1)
    return jnp.where(rows == cols, 1.0, 0.0).astype(f32)


def put_block(i, value, hi_ref, lo_ref, pair, whole_ref=None):
    cells = (((value, 0, 0),), ((value, 0, 1), (-value.T, 1, 0)), ((value, 1, 1),))[i]
    for cell, r, c in cells:
        hi, lo = split(cell)
        hi_ref[pair, r * BLK : (r + 1) * BLK, c * BLK : (c + 1) * BLK] = hi
        lo_ref[pair, r * BLK : (r + 1) * BLK, c * BLK : (c + 1) * BLK] = lo
        if whole_ref is not None:
            whole_ref[2 * pair + c, r] = cell


def rounds_kernel(
    n_row, n_col, rows,
    plan_ref, x_ref, xh_ref, xl_ref, qh_ref, ql_ref,
    xv, nv, zsend, zrecv, gram, sq, part_send, part_recv, rs_src, rs_recv, ag, gmat, cmat, qv, qhi, qlo, qf,
    esend, erecv, zearly, qz, qz_all, qz_other,
    load_sem, part_s, part_r, rs_s, rs_r, ag_s, ag_r, q_s, q_r, z_s, z_r,
    e_s, e_r, qz_s, qz_r, qa_s, qa_r, qp_s, qp_r,
):
    chips = n_row // 2
    crow = BLK // chips
    row, z = lax.axis_index("row"), lax.axis_index("col")
    core, chip = lax.rem(row, 2), row // 2
    other = 1 - core
    partner = (chip * 2 + other, z)
    z_up, z_down = lax.rem(z + 1, n_col), lax.rem(z + n_col - 1, n_col)
    unit = rows // 8
    late = [(0, 2 * unit), (2 * unit, unit), (3 * unit, unit)]
    early, n_early = 4 * unit, 4 * unit

    side = math.isqrt(chips)
    cx, cy = chip // side, lax.rem(chip, side)

    def hops(offset):
        return min(offset, side - offset)

    far_first = sorted(
        [(dx, dy) for dx in range(side) for dy in range(side) if (dx, dy) != (0, 0)],
        key=lambda d: -hops(d[0]) - hops(d[1]),
    )
    peers = []
    for dx, dy in far_first:
        t = lax.rem(cx + dx, side) * side + lax.rem(cy + dy, side)
        peers.append((t, (t * 2 + core, z)))

    loads = []
    for i, p in enumerate((other, core)):
        for h in range(2):
            cols = pl.ds(pl.multiple_of((2 * p + h) * BLK, BLK), BLK)
            loads.append(pltpu.make_async_copy(x_ref.at[:, cols], xv.at[2 * p + h], load_sem.at[2 * i + h]))
            loads[-1].start()

    barrier = pltpu.get_barrier_semaphore()

    for dev in [dev for _, dev in peers] + [(row, z_up), (row, z_down), partner]:
        pl.semaphore_signal(barrier, inc=1, device_id=dev, device_id_type=MESH)

    def gram_step(p, start, step_rows, keep=False):
        rs = pl.ds(start, step_rows)
        lead, mate = xv[2 * p, rs, :], xv[2 * p + 1, rs, :]
        lh, ll = split(lead)
        mh, ml = split(mate)
        if keep:
            for h, hi, lo in ((0, lh, ll), (1, mh, ml)):
                cols = pl.ds(pl.multiple_of((2 * p + h) * BLK, BLK), BLK)
                xh_ref[rs, cols] = hi
                xl_ref[rs, cols] = lo
        gram[p] += mm_t(lh, mh) + (mm_t(lh, ml) + mm_t(ll, mh))
        sq[p, 0] += jnp.sum((lead * lead).reshape(step_rows // 8, 8, BLK), axis=0)
        sq[p, 1] += jnp.sum((mate * mate).reshape(step_rows // 8, 8, BLK), axis=0)

    def squares(p):
        lead_sq = jnp.sum(sq[p, 0], axis=0, keepdims=True)
        mate_sq = jnp.sum(sq[p, 1], axis=0, keepdims=True)
        return jnp.concatenate(
            [lead_sq[:, :HALF], lead_sq[:, HALF:], mate_sq[:, :HALF], mate_sq[:, HALF:], jnp.zeros((4, HALF), f32)],
            axis=0,
        )

    def part_copy(rnd):
        return pltpu.make_async_remote_copy(
            part_send.at[rnd], part_recv.at[rnd], part_s.at[rnd], part_r.at[rnd], device_id=partner, device_id_type=MESH
        )

    def fill_part(rnd):
        part_send[rnd, 0:BLK, :] = gram[other, :, 0:HALF]
        part_send[rnd, BLK : 2 * BLK, :] = gram[other, :, HALF:BLK]
        part_send[rnd, 2 * BLK : 2 * BLK + 8, :] = squares(other)

    def reduce_gram(rnd):
        own_sq = squares(core)
        part_copy(rnd).wait()
        left = gram[core, :, 0:HALF] + part_recv[rnd, 0:BLK, :]
        right = gram[core, :, HALF:BLK] + part_recv[rnd, BLK : 2 * BLK, :]
        both_sq = own_sq + part_recv[rnd, 2 * BLK : 2 * BLK + 8, :]
        rs_src[rnd, :, 0:crow, :] = left.reshape(chips, crow, HALF)
        rs_src[rnd, :, crow : 2 * crow, :] = right.reshape(chips, crow, HALF)
        rs_src[rnd, :, 2 * crow : 2 * crow + 8, :] = jnp.broadcast_to(both_sq[None], (chips, 8, HALF))

        sent = crow * 2 + 4

        def rs_copy(k, t, dev, source):
            return pltpu.make_async_remote_copy(
                rs_src.at[rnd, t, 0:sent], rs_recv.at[rnd, source, 0:sent], rs_s.at[rnd, k], rs_r.at[rnd, source],
                device_id=dev, device_id_type=MESH,
            )

        def ag_copy(k, dev, source):
            return pltpu.make_async_remote_copy(
                ag.at[rnd, source], ag.at[rnd, source], ag_s.at[rnd, k], ag_r.at[rnd, source],
                device_id=dev, device_id_type=MESH,
            )

        for k, (t, dev) in enumerate(peers):
            rs_copy(k, t, dev, chip).start()
        rs_recv[rnd, chip] = rs_src[rnd, chip]
        for k, (t, dev) in enumerate(peers):
            rs_copy(k, t, dev, t).wait_recv()
        total = jnp.sum(rs_recv[rnd], axis=0)
        ag[rnd, chip] = total[0 : 2 * crow]
        for k, (t, dev) in enumerate(peers):
            ag_copy(k, dev, chip).start()
        for k, (t, dev) in enumerate(peers):
            rs_copy(k, t, dev, chip).wait_send()
        for k, (t, dev) in enumerate(peers):
            ag_copy(k, dev, t).wait_recv()
        for k, (t, dev) in enumerate(peers):
            ag_copy(k, dev, chip).wait_send()
        return total[2 * crow : 2 * crow + 8]

    def rotation(rnd, sums, *refs):
        lead_sq = jnp.concatenate([sums[0:1], sums[1:2]], axis=1)
        mate_sq = jnp.concatenate([sums[2:3], sums[3:4]], axis=1)
        lead_col = jnp.broadcast_to(lead_sq, (8, BLK)).T[:, 0:1]
        cross = jnp.concatenate(
            [ag[rnd, :, 0:crow, :].reshape(BLK, HALF), ag[rnd, :, crow : 2 * crow, :].reshape(BLK, HALF)], axis=1
        )
        cmat[...] = cross / (lead_col + mate_sq + EPS)
        ident = eye()
        gmat[...] = ident + 0.25 * full(cmat[...], cmat[...], ((1,), (1,)))
        scale = 2.0 / (1.0 + BOUND)
        radius = (BOUND - 1.0) / (BOUND + 1.0)
        res = split(ident - scale * gmat[...])
        inv = None
        for k in range(STEPS):
            s = 2.0 / (2.0 - radius * radius)
            radius = radius * radius / (2.0 - radius * radius)
            if k < STEPS - 1:
                square = mm3(res, res)
            if k == 0:
                inv = (s * scale) * (ident + (res[0].astype(f32) + res[1].astype(f32)))
            else:
                inv = s * (inv + mm3(split(inv), res))
            if k < STEPS - 1:
                res = split(s * square + (1.0 - s) * ident)
        inv_parts = split(inv)
        inv = inv + mm3(inv_parts, split(ident - mm3(split(gmat[...]), inv_parts)))
        w = full(inv, cmat[...], ((1,), (0,)))
        err = split(ident - full(inv, gmat[...], ((1,), (0,))))
        inv = inv + mm3(err, split(inv))
        send_block(rnd, 0, 2.0 * inv - ident, refs)
        w = w + mm3(err, split(w))
        send_block(rnd, 1, w, refs)
        send_block(rnd, 2, ident - 0.5 * full(cmat[...], w, ((0,), (0,))), refs)

    def send_block(rnd, i, value, refs):
        qv[rnd, core, i] = value
        q_copy(rnd, core, i).start()
        put_block(i, value, refs[0], refs[1], core, *refs[2:])

    def receive_blocks(rnd, *refs):
        for i in range(3):
            q_copy(rnd, other, i).wait_recv()
            put_block(i, qv[rnd, other, i], refs[0], refs[1], other, *refs[2:])
        for i in range(3):
            q_copy(rnd, core, i).wait_send()

    def q_copy(rnd, p, i):
        return pltpu.make_async_remote_copy(
            qv.at[rnd, p, i], qv.at[rnd, p, i], q_s.at[rnd, i], q_r.at[rnd, i], device_id=partner, device_id_type=MESH
        )

    def rotate(p, start, step_rows):
        rs = pl.ds(start, step_rows)
        x = jnp.concatenate([xv[2 * p, rs, :], xv[2 * p + 1, rs, :]], axis=1)
        xh, xl = split(x)
        for h in range(2):
            cols = slice(h * BLK, (h + 1) * BLK)
            nv[2 * p + h, rs, :] = mm3((xh, xl), (qhi[p, :, cols], qlo[p, :, cols]))

    up_slot = down_slot = jnp.int32(0)
    for j in range(4):
        above, below = plan_ref[1, z_up * 4 + j], plan_ref[1, z_down * 4 + j]
        up_slot = jnp.where(above // 4 == z, above - 4 * z, up_slot)
        down_slot = jnp.where(below // 4 == z, below - 4 * z, down_slot)
    origin = [plan_ref[1, z * 4 + j] for j in range(4)]

    def z_copy(way, i):
        rs = pl.ds(*late[i])
        return pltpu.make_async_remote_copy(
            zsend.at[way, rs, :], zrecv.at[way, rs, :], z_s.at[way, i], z_r.at[way, i],
            device_id=(row, z_up if way == 0 else z_down), device_id_type=MESH,
        )

    def early_copy(way):
        return pltpu.make_async_remote_copy(
            esend.at[way], erecv.at[way], e_s.at[way], e_r.at[way],
            device_id=(row, z_up if way == 0 else z_down), device_id_type=MESH,
        )

    def share_copy(way):
        return pltpu.make_async_remote_copy(
            qz.at[way], qz_all.at[chip, way], qz_s.at[way], qz_r.at[way],
            device_id=(row, z_up if way == 0 else z_down), device_id_type=MESH,
        )

    def share_gather(k, dev, source):
        return pltpu.make_async_remote_copy(
            qz_all.at[source], qz_all.at[source], qa_s.at[k], qa_r.at[source], device_id=dev, device_id_type=MESH
        )

    def share_swap():
        return pltpu.make_async_remote_copy(
            qz_all, qz_other, qp_s.at[0], qp_r.at[0], device_id=partner, device_id_type=MESH
        )

    gram[...] = jnp.zeros_like(gram)
    sq[...] = jnp.zeros_like(sq)
    loads[0].wait()
    loads[1].wait()
    for start in range(0, rows, 2 * unit):
        gram_step(other, start, 2 * unit)
    loads[2].wait()
    loads[3].wait()
    for way, slot in enumerate((up_slot, down_slot)):
        for h in range(2):
            esend[way, h] = xv[(slot // 2) * 2 + h, pl.ds(early, n_early), :]
    fill_part(0)
    for start in range(0, rows, 2 * unit):
        gram_step(core, start, 2 * unit)
    pl.semaphore_wait(barrier, chips + 2)
    part_copy(0).start()
    for way in range(2):
        early_copy(way).start()
    rotation(0, reduce_gram(0), qhi, qlo, qf)
    for start, size in late:
        rotate(core, start, size)
    receive_blocks(0, qhi, qlo, qf)
    for way, slot in enumerate((up_slot, down_slot)):
        qz[way] = qf[slot, core, pl.ds(pl.multiple_of(chip * crow, crow), crow), :]
        share_copy(way).start()
    for i, (start, size) in enumerate(late):
        rotate(other, start, size)
        rs = pl.ds(start, size)
        zsend[0, rs, :] = nv[up_slot, rs, :]
        z_copy(0, i).start()
        zsend[1, rs, :] = nv[down_slot, rs, :]
        z_copy(1, i).start()
    for way in range(2):
        share_copy(way).wait_recv()
    for k, (_, dev) in enumerate(peers):
        share_gather(k, dev, chip).start()
    rotate(core, early, n_early)
    rotate(other, early, n_early)

    gram[...] = jnp.zeros_like(gram)
    sq[...] = jnp.zeros_like(sq)

    def place(start, size, lower, upper):
        rs = pl.ds(start, size)
        for j in range(4):
            home = origin[j] // 4
            own = nv[jnp.clip(origin[j] - 4 * z, 0, 3), rs, :]
            xv[j, rs, :] = jnp.where(home == z, own, jnp.where(home < z, lower[...], upper[...]))

    def arrive(i):
        z_copy(0, i).wait_recv()
        z_copy(1, i).wait_recv()
        rs = pl.ds(*late[i])
        place(*late[i], zrecv.at[0, rs, :], zrecv.at[1, rs, :])

    arrive(0)
    gram_step(other, *late[0], True)
    gram_step(core, *late[0], True)
    for k, (t, dev) in enumerate(peers):
        share_gather(k, dev, t).wait_recv()
    share_swap().start()
    for way in range(2):
        early_copy(way).wait_recv()
    for way in range(2):
        part = qz_all[:, way].reshape(BLK, BLK)
        zearly[way] = mm3(split(erecv[way, core]), split(part))
    arrive(1)
    gram_step(other, *late[1], True)
    gram_step(core, *late[1], True)
    share_swap().wait_recv()
    for way in range(2):
        part = qz_other[:, way].reshape(BLK, BLK)
        zearly[way] += mm3(split(erecv[way, other]), split(part))
    place(early, n_early, zearly.at[0], zearly.at[1])
    gram_step(other, early, n_early, True)
    gram_step(core, early, n_early, True)
    arrive(2)
    gram_step(other, *late[2], True)
    fill_part(1)
    part_copy(1).start()
    gram_step(core, *late[2], True)
    for way in range(2):
        for i in range(len(late)):
            z_copy(way, i).wait_send()
        early_copy(way).wait_send()
        share_copy(way).wait_send()
    for k, (_, dev) in enumerate(peers):
        share_gather(k, dev, chip).wait_send()
    share_swap().wait_send()
    rotation(1, reduce_gram(1), qh_ref, ql_ref)
    receive_blocks(1, qh_ref, ql_ref)


def two_rounds(plan, x, n_row, n_col):
    rows = x.shape[0]
    n_early = rows // 2
    chips = n_row // 2
    crow = BLK // chips
    dma = pltpu.SemaphoreType.DMA
    return pl.pallas_call(
        functools.partial(rounds_kernel, n_row, n_col, rows),
        out_shape=[jax.ShapeDtypeStruct(x.shape, bf16)] * 2 + [jax.ShapeDtypeStruct((2, 2 * BLK, 2 * BLK), bf16)] * 2,
        in_specs=[pl.BlockSpec(memory_space=pltpu.SMEM), pl.BlockSpec(memory_space=pl.ANY)],
        out_specs=[pl.BlockSpec(memory_space=pltpu.VMEM)] * 4,
        scratch_shapes=[
            pltpu.VMEM((4, rows, BLK), f32),
            pltpu.VMEM((4, rows, BLK), f32),
            pltpu.VMEM((2, rows, BLK), f32),
            pltpu.VMEM((2, rows, BLK), f32),
            pltpu.VMEM((2, BLK, BLK), f32),
            pltpu.VMEM((2, 2, 8, BLK), f32),
            pltpu.VMEM((2, 2 * BLK + 8, HALF), f32),
            pltpu.VMEM((2, 2 * BLK + 8, HALF), f32),
            pltpu.VMEM((2, chips, 2 * crow + 8, HALF), f32),
            pltpu.VMEM((2, chips, 2 * crow + 8, HALF), f32),
            pltpu.VMEM((2, chips, 2 * crow, HALF), f32),
            pltpu.VMEM((BLK, BLK), f32),
            pltpu.VMEM((BLK, BLK), f32),
            pltpu.VMEM((2, 2, 3, BLK, BLK), f32),
            pltpu.VMEM((2, 2 * BLK, 2 * BLK), bf16),
            pltpu.VMEM((2, 2 * BLK, 2 * BLK), bf16),
            pltpu.VMEM((4, 2, BLK, BLK), f32),
            pltpu.VMEM((2, 2, n_early, BLK), f32),
            pltpu.VMEM((2, 2, n_early, BLK), f32),
            pltpu.VMEM((2, n_early, BLK), f32),
            pltpu.VMEM((2, crow, BLK), f32),
            pltpu.VMEM((chips, 2, crow, BLK), f32),
            pltpu.VMEM((chips, 2, crow, BLK), f32),
            dma((4,)),
            dma((2,)), dma((2,)),
            dma((2, chips)), dma((2, chips)),
            dma((2, chips)), dma((2, chips)),
            dma((2, 3)), dma((2, 3)),
            dma((2, 3)), dma((2, 3)),
            dma((2,)), dma((2,)),
            dma((2,)), dma((2,)),
            dma((chips,)), dma((chips,)),
            dma((1,)), dma((1,)),
        ],
        compiler_params=pltpu.CompilerParams(collective_id=0, has_side_effects=True, vmem_limit_bytes=46 << 20),
    )(plan, x)


def rotate_kernel(step_rows, xh_ref, xl_ref, qh_ref, ql_ref, o_ref):
    rs = pl.ds(pl.multiple_of(pl.program_id(0) * step_rows, step_rows), step_rows)
    for p in range(2):
        pair = slice(2 * p * BLK, (2 * p + 2) * BLK)
        x = xh_ref[rs, pair], xl_ref[rs, pair]
        for h in range(2):
            cols = slice(h * BLK, (h + 1) * BLK)
            o_ref[:, (2 * p + h) * BLK : (2 * p + h + 1) * BLK] = mm3(x, (qh_ref[p, :, cols], ql_ref[p, :, cols]))


def last_rotation(xh, xl, qh, ql):
    rows = xh.shape[0]
    step_rows = rows // 4
    return pl.pallas_call(
        functools.partial(rotate_kernel, step_rows),
        grid=(rows // step_rows,),
        out_shape=jax.ShapeDtypeStruct(xh.shape, f32),
        in_specs=[pl.BlockSpec(memory_space=pltpu.VMEM)] * 4,
        out_specs=pl.BlockSpec((step_rows, 4 * BLK), lambda i: (i, 0)),
        compiler_params=pltpu.CompilerParams(vmem_limit_bytes=20 << 20),
    )(xh, xl, qh, ql)


def shards(n_row, n_col, activations, plan):
    return last_rotation(*two_rounds(plan, activations, n_row, n_col))


def solution(mesh):
    placed = (P("row", "col"), P())
    return jax.shard_map(
        functools.partial(shards, mesh.shape["row"], mesh.shape["col"]),
        mesh=mesh, in_specs=placed, out_specs=P("row", "col"), check_vma=False,
    )
```

```python
import functools
import math

import jax
import jax.numpy as jnp
from jax import lax
from jax.experimental import pallas as pl
from jax.experimental.pallas import tpu as pltpu
from jax.sharding import PartitionSpec as P

BLK = 256
HALF = 128
EPS = 1e-6
STEPS = 7
BOUND = 1.02 * (1.0 + (BLK / 2) ** 2 / 4)
MESH = pl.DeviceIdType.MESH
HIGHEST = lax.Precision.HIGHEST
f32, bf16 = jnp.float32, jnp.bfloat16


def split(value):
    hi = value.astype(bf16)
    return hi, (value - hi.astype(f32)).astype(bf16)


def mm(a, b):
    return lax.dot_general(a, b, (((1,), (0,)), ((), ())), preferred_element_type=f32)


def mm_t(a, b):
    return lax.dot_general(a, b, (((0,), (0,)), ((), ())), preferred_element_type=f32)


def mm3(a, b):
    return mm(a[0], b[0]) + (mm(a[0], b[1]) + mm(a[1], b[0]))


def full(a, b, dims):
    return lax.dot_general(a, b, (dims, ((), ())), precision=HIGHEST, preferred_element_type=f32)


def eye():
    rows = lax.broadcasted_iota(jnp.int32, (BLK, BLK), 0)
    cols = lax.broadcasted_iota(jnp.int32, (BLK, BLK), 1)
    return jnp.where(rows == cols, 1.0, 0.0).astype(f32)


def put_block(i, value, hi_ref, lo_ref, pair, whole_ref=None):
    cells = (((value, 0, 0),), ((value, 0, 1), (-value.T, 1, 0)), ((value, 1, 1),))[i]
    for cell, r, c in cells:
        hi, lo = split(cell)
        hi_ref[pair, r * BLK : (r + 1) * BLK, c * BLK : (c + 1) * BLK] = hi
        lo_ref[pair, r * BLK : (r + 1) * BLK, c * BLK : (c + 1) * BLK] = lo
        if whole_ref is not None:
            whole_ref[2 * pair + c, r] = cell


def rounds_kernel(
    n_row, n_col, rows,
    plan_ref, x_ref, xh_ref, xl_ref, qh_ref, ql_ref,
    xv, nv, zsend, zrecv, gram, sq, part_send, part_recv, rs_src, rs_recv, ag, gmat, cmat, qv, qhi, qlo, qf,
    esend, erecv, zearly, qz, qz_all, qz_other,
    load_sem, part_s, part_r, rs_s, rs_r, ag_s, ag_r, q_s, q_r, z_s, z_r,
    e_s, e_r, qz_s, qz_r, qa_s, qa_r, qp_s, qp_r,
):
    chips = n_row // 2
    crow = BLK // chips
    row, z = lax.axis_index("row"), lax.axis_index("col")
    core, chip = lax.rem(row, 2), row // 2
    other = 1 - core
    partner = (chip * 2 + other, z)
    z_up, z_down = lax.rem(z + 1, n_col), lax.rem(z + n_col - 1, n_col)
    unit = rows // 8
    late = [(0, 2 * unit), (2 * unit, unit), (3 * unit, unit)]
    early, n_early = 4 * unit, 4 * unit

    side = math.isqrt(chips)
    cx, cy = chip // side, lax.rem(chip, side)

    def hops(offset):
        return min(offset, side - offset)

    far_first = sorted(
        [(dx, dy) for dx in range(side) for dy in range(side) if (dx, dy) != (0, 0)],
        key=lambda d: -hops(d[0]) - hops(d[1]),
    )
    peers = []
    for dx, dy in far_first:
        t = lax.rem(cx + dx, side) * side + lax.rem(cy + dy, side)
        peers.append((t, (t * 2 + core, z)))

    loads = []
    for i, p in enumerate((other, core)):
        for h in range(2):
            cols = pl.ds(pl.multiple_of((2 * p + h) * BLK, BLK), BLK)
            loads.append(pltpu.make_async_copy(x_ref.at[:, cols], xv.at[2 * p + h], load_sem.at[2 * i + h]))
            loads[-1].start()

    barrier = pltpu.get_barrier_semaphore()

    for dev in [dev for _, dev in peers] + [(row, z_up), (row, z_down), partner]:
        pl.semaphore_signal(barrier, inc=1, device_id=dev, device_id_type=MESH)

    def gram_step(p, start, step_rows, keep=False):
        rs = pl.ds(start, step_rows)
        lead, mate = xv[2 * p, rs, :], xv[2 * p + 1, rs, :]
        lh, ll = split(lead)
        mh, ml = split(mate)
        if keep:
            for h, hi, lo in ((0, lh, ll), (1, mh, ml)):
                cols = pl.ds(pl.multiple_of((2 * p + h) * BLK, BLK), BLK)
                xh_ref[rs, cols] = hi
                xl_ref[rs, cols] = lo
        gram[p] += mm_t(lh, mh) + (mm_t(lh, ml) + mm_t(ll, mh))
        sq[p, 0] += jnp.sum((lead * lead).reshape(step_rows // 8, 8, BLK), axis=0)
        sq[p, 1] += jnp.sum((mate * mate).reshape(step_rows // 8, 8, BLK), axis=0)

    def squares(p):
        lead_sq = jnp.sum(sq[p, 0], axis=0, keepdims=True)
        mate_sq = jnp.sum(sq[p, 1], axis=0, keepdims=True)
        return jnp.concatenate(
            [lead_sq[:, :HALF], lead_sq[:, HALF:], mate_sq[:, :HALF], mate_sq[:, HALF:], jnp.zeros((4, HALF), f32)],
            axis=0,
        )

    def part_copy(rnd):
        return pltpu.make_async_remote_copy(
            part_send.at[rnd], part_recv.at[rnd], part_s.at[rnd], part_r.at[rnd], device_id=partner, device_id_type=MESH
        )

    def fill_part(rnd):
        part_send[rnd, 0:BLK, :] = gram[other, :, 0:HALF]
        part_send[rnd, BLK : 2 * BLK, :] = gram[other, :, HALF:BLK]
        part_send[rnd, 2 * BLK : 2 * BLK + 8, :] = squares(other)

    def reduce_gram(rnd):
        own_sq = squares(core)
        part_copy(rnd).wait()
        left = gram[core, :, 0:HALF] + part_recv[rnd, 0:BLK, :]
        right = gram[core, :, HALF:BLK] + part_recv[rnd, BLK : 2 * BLK, :]
        both_sq = own_sq + part_recv[rnd, 2 * BLK : 2 * BLK + 8, :]
        rs_src[rnd, :, 0:crow, :] = left.reshape(chips, crow, HALF)
        rs_src[rnd, :, crow : 2 * crow, :] = right.reshape(chips, crow, HALF)
        rs_src[rnd, :, 2 * crow : 2 * crow + 8, :] = jnp.broadcast_to(both_sq[None], (chips, 8, HALF))

        sent = crow * 2 + 4

        def rs_copy(k, t, dev, source):
            return pltpu.make_async_remote_copy(
                rs_src.at[rnd, t, 0:sent], rs_recv.at[rnd, source, 0:sent], rs_s.at[rnd, k], rs_r.at[rnd, source],
                device_id=dev, device_id_type=MESH,
            )

        def ag_copy(k, dev, source):
            return pltpu.make_async_remote_copy(
                ag.at[rnd, source], ag.at[rnd, source], ag_s.at[rnd, k], ag_r.at[rnd, source],
                device_id=dev, device_id_type=MESH,
            )

        for k, (t, dev) in enumerate(peers):
            rs_copy(k, t, dev, chip).start()
        rs_recv[rnd, chip] = rs_src[rnd, chip]
        for k, (t, dev) in enumerate(peers):
            rs_copy(k, t, dev, t).wait_recv()
        total = jnp.sum(rs_recv[rnd], axis=0)
        ag[rnd, chip] = total[0 : 2 * crow]
        for k, (t, dev) in enumerate(peers):
            ag_copy(k, dev, chip).start()
        for k, (t, dev) in enumerate(peers):
            rs_copy(k, t, dev, chip).wait_send()
        for k, (t, dev) in enumerate(peers):
            ag_copy(k, dev, t).wait_recv()
        for k, (t, dev) in enumerate(peers):
            ag_copy(k, dev, chip).wait_send()
        return total[2 * crow : 2 * crow + 8]

    def rotation(rnd, sums, *refs):
        lead_sq = jnp.concatenate([sums[0:1], sums[1:2]], axis=1)
        mate_sq = jnp.concatenate([sums[2:3], sums[3:4]], axis=1)
        lead_col = jnp.broadcast_to(lead_sq, (8, BLK)).T[:, 0:1]
        cross = jnp.concatenate(
            [ag[rnd, :, 0:crow, :].reshape(BLK, HALF), ag[rnd, :, crow : 2 * crow, :].reshape(BLK, HALF)], axis=1
        )
        cmat[...] = cross / (lead_col + mate_sq + EPS)
        ident = eye()
        gmat[...] = ident + 0.25 * full(cmat[...], cmat[...], ((1,), (1,)))
        scale = 2.0 / (1.0 + BOUND)
        radius = (BOUND - 1.0) / (BOUND + 1.0)
        res = split(ident - scale * gmat[...])
        inv = None
        for k in range(STEPS):
            s = 2.0 / (2.0 - radius * radius)
            radius = radius * radius / (2.0 - radius * radius)
            if k < STEPS - 1:
                square = mm3(res, res)
            if k == 0:
                inv = (s * scale) * (ident + (res[0].astype(f32) + res[1].astype(f32)))
            else:
                inv = s * (inv + mm3(split(inv), res))
            if k < STEPS - 1:
                res = split(s * square + (1.0 - s) * ident)
        inv_parts = split(inv)
        inv = inv + mm3(inv_parts, split(ident - mm3(split(gmat[...]), inv_parts)))
        w = full(inv, cmat[...], ((1,), (0,)))
        err = split(ident - full(inv, gmat[...], ((1,), (0,))))
        inv = inv + mm3(err, split(inv))
        send_block(rnd, 0, 2.0 * inv - ident, refs)
        w = w + mm3(err, split(w))
        send_block(rnd, 1, w, refs)
        send_block(rnd, 2, ident - 0.5 * full(cmat[...], w, ((0,), (0,))), refs)

    def send_block(rnd, i, value, refs):
        qv[rnd, core, i] = value
        q_copy(rnd, core, i).start()
        put_block(i, value, refs[0], refs[1], core, *refs[2:])

    def receive_blocks(rnd, *refs):
        for i in range(3):
            q_copy(rnd, other, i).wait_recv()
            put_block(i, qv[rnd, other, i], refs[0], refs[1], other, *refs[2:])
        for i in range(3):
            q_copy(rnd, core, i).wait_send()

    def q_copy(rnd, p, i):
        return pltpu.make_async_remote_copy(
            qv.at[rnd, p, i], qv.at[rnd, p, i], q_s.at[rnd, i], q_r.at[rnd, i], device_id=partner, device_id_type=MESH
        )

    def rotate(p, start, step_rows):
        rs = pl.ds(start, step_rows)
        x = jnp.concatenate([xv[2 * p, rs, :], xv[2 * p + 1, rs, :]], axis=1)
        xh, xl = split(x)
        for h in range(2):
            cols = slice(h * BLK, (h + 1) * BLK)
            nv[2 * p + h, rs, :] = mm3((xh, xl), (qhi[p, :, cols], qlo[p, :, cols]))

    up_slot = down_slot = jnp.int32(0)
    for j in range(4):
        above, below = plan_ref[1, z_up * 4 + j], plan_ref[1, z_down * 4 + j]
        up_slot = jnp.where(above // 4 == z, above - 4 * z, up_slot)
        down_slot = jnp.where(below // 4 == z, below - 4 * z, down_slot)

    def z_copy(way, i):
        rs = pl.ds(*late[i])
        return pltpu.make_async_remote_copy(
            zsend.at[way, rs, :], zrecv.at[way, rs, :], z_s.at[way, i], z_r.at[way, i],
            device_id=(row, z_up if way == 0 else z_down), device_id_type=MESH,
        )

    def early_copy(way):
        return pltpu.make_async_remote_copy(
            esend.at[way], erecv.at[way], e_s.at[way], e_r.at[way],
            device_id=(row, z_up if way == 0 else z_down), device_id_type=MESH,
        )

    def share_copy(way):
        return pltpu.make_async_remote_copy(
            qz.at[way], qz_all.at[chip, way], qz_s.at[way], qz_r.at[way],
            device_id=(row, z_up if way == 0 else z_down), device_id_type=MESH,
        )

    def share_gather(k, dev, source):
        return pltpu.make_async_remote_copy(
            qz_all.at[source], qz_all.at[source], qa_s.at[k], qa_r.at[source], device_id=dev, device_id_type=MESH
        )

    def share_swap():
        return pltpu.make_async_remote_copy(
            qz_all, qz_other, qp_s.at[0], qp_r.at[0], device_id=partner, device_id_type=MESH
        )

    gram[...] = jnp.zeros_like(gram)
    sq[...] = jnp.zeros_like(sq)
    loads[0].wait()
    loads[1].wait()
    for start in range(0, rows, 2 * unit):
        gram_step(other, start, 2 * unit)
    fill_part(0)
    loads[2].wait()
    loads[3].wait()
    for way, slot in enumerate((up_slot, down_slot)):
        for h in range(2):
            esend[way, h] = xv[(slot // 2) * 2 + h, pl.ds(early, n_early), :]
    pl.semaphore_wait(barrier, chips + 2)
    for way in range(2):
        early_copy(way).start()
    part_copy(0).start()
    for start in range(0, rows, 2 * unit):
        gram_step(core, start, 2 * unit)
    rotation(0, reduce_gram(0), qhi, qlo, qf)
    for start, size in late:
        rotate(core, start, size)
    receive_blocks(0, qhi, qlo, qf)
    for way, slot in enumerate((up_slot, down_slot)):
        qz[way] = qf[slot, core, pl.ds(pl.multiple_of(chip * crow, crow), crow), :]
        share_copy(way).start()
    for i, (start, size) in enumerate(late):
        rotate(other, start, size)
        rs = pl.ds(start, size)
        zsend[0, rs, :] = nv[up_slot, rs, :]
        z_copy(0, i).start()
        zsend[1, rs, :] = nv[down_slot, rs, :]
        z_copy(1, i).start()
    for way in range(2):
        share_copy(way).wait_recv()
    for k, (_, dev) in enumerate(peers):
        share_gather(k, dev, chip).start()
    rotate(core, early, n_early)
    rotate(other, early, n_early)

    gram[...] = jnp.zeros_like(gram)
    sq[...] = jnp.zeros_like(sq)

    def place(p, start, size, lower, upper):
        rs = pl.ds(start, size)
        for h in range(2):
            origin = plan_ref[1, z * 4 + 2 * p + h]
            home = origin // 4
            own = nv[jnp.clip(origin - 4 * z, 0, 3), rs, :]
            xv[2 * p + h, rs, :] = jnp.where(home == z, own, jnp.where(home < z, lower[...], upper[...]))
        gram_step(p, start, size, True)

    def arrive(i):
        z_copy(0, i).wait_recv()
        z_copy(1, i).wait_recv()

    def place_late(p, i):
        rs = pl.ds(*late[i])
        place(p, *late[i], zrecv.at[0, rs, :], zrecv.at[1, rs, :])

    arrive(0)
    place_late(other, 0)
    place_late(core, 0)
    for k, (t, dev) in enumerate(peers):
        share_gather(k, dev, t).wait_recv()
    share_swap().start()
    for way in range(2):
        early_copy(way).wait_recv()
    for way in range(2):
        part = qz_all[:, way].reshape(BLK, BLK)
        zearly[way] = mm3(split(erecv[way, core]), split(part))
    arrive(1)
    place_late(other, 1)
    place_late(core, 1)
    share_swap().wait_recv()
    for way in range(2):
        part = qz_other[:, way].reshape(BLK, BLK)
        zearly[way] += mm3(split(erecv[way, other]), split(part))
    place(other, early, n_early, zearly.at[0], zearly.at[1])
    place(core, early, n_early, zearly.at[0], zearly.at[1])
    arrive(2)
    place_late(other, 2)
    fill_part(1)
    part_copy(1).start()
    place_late(core, 2)
    for way in range(2):
        for i in range(len(late)):
            z_copy(way, i).wait_send()
        early_copy(way).wait_send()
        share_copy(way).wait_send()
    for k, (_, dev) in enumerate(peers):
        share_gather(k, dev, chip).wait_send()
    share_swap().wait_send()
    rotation(1, reduce_gram(1), qh_ref, ql_ref)
    receive_blocks(1, qh_ref, ql_ref)


def two_rounds(plan, x, n_row, n_col):
    rows = x.shape[0]
    n_early = rows // 2
    chips = n_row // 2
    crow = BLK // chips
    dma = pltpu.SemaphoreType.DMA
    return pl.pallas_call(
        functools.partial(rounds_kernel, n_row, n_col, rows),
        out_shape=[jax.ShapeDtypeStruct(x.shape, bf16)] * 2 + [jax.ShapeDtypeStruct((2, 2 * BLK, 2 * BLK), bf16)] * 2,
        in_specs=[pl.BlockSpec(memory_space=pltpu.SMEM), pl.BlockSpec(memory_space=pl.ANY)],
        out_specs=[pl.BlockSpec(memory_space=pltpu.VMEM)] * 4,
        scratch_shapes=[
            pltpu.VMEM((4, rows, BLK), f32),
            pltpu.VMEM((4, rows, BLK), f32),
            pltpu.VMEM((2, rows, BLK), f32),
            pltpu.VMEM((2, rows, BLK), f32),
            pltpu.VMEM((2, BLK, BLK), f32),
            pltpu.VMEM((2, 2, 8, BLK), f32),
            pltpu.VMEM((2, 2 * BLK + 8, HALF), f32),
            pltpu.VMEM((2, 2 * BLK + 8, HALF), f32),
            pltpu.VMEM((2, chips, 2 * crow + 8, HALF), f32),
            pltpu.VMEM((2, chips, 2 * crow + 8, HALF), f32),
            pltpu.VMEM((2, chips, 2 * crow, HALF), f32),
            pltpu.VMEM((BLK, BLK), f32),
            pltpu.VMEM((BLK, BLK), f32),
            pltpu.VMEM((2, 2, 3, BLK, BLK), f32),
            pltpu.VMEM((2, 2 * BLK, 2 * BLK), bf16),
            pltpu.VMEM((2, 2 * BLK, 2 * BLK), bf16),
            pltpu.VMEM((4, 2, BLK, BLK), f32),
            pltpu.VMEM((2, 2, n_early, BLK), f32),
            pltpu.VMEM((2, 2, n_early, BLK), f32),
            pltpu.VMEM((2, n_early, BLK), f32),
            pltpu.VMEM((2, crow, BLK), f32),
            pltpu.VMEM((chips, 2, crow, BLK), f32),
            pltpu.VMEM((chips, 2, crow, BLK), f32),
            dma((4,)),
            dma((2,)), dma((2,)),
            dma((2, chips)), dma((2, chips)),
            dma((2, chips)), dma((2, chips)),
            dma((2, 3)), dma((2, 3)),
            dma((2, 3)), dma((2, 3)),
            dma((2,)), dma((2,)),
            dma((2,)), dma((2,)),
            dma((chips,)), dma((chips,)),
            dma((1,)), dma((1,)),
        ],
        compiler_params=pltpu.CompilerParams(collective_id=0, has_side_effects=True, vmem_limit_bytes=46 << 20),
    )(plan, x)


def rotate_kernel(step_rows, xh_ref, xl_ref, qh_ref, ql_ref, o_ref):
    rs = pl.ds(pl.multiple_of(pl.program_id(0) * step_rows, step_rows), step_rows)
    for p in range(2):
        pair = slice(2 * p * BLK, (2 * p + 2) * BLK)
        x = xh_ref[rs, pair], xl_ref[rs, pair]
        for h in range(2):
            cols = slice(h * BLK, (h + 1) * BLK)
            o_ref[:, (2 * p + h) * BLK : (2 * p + h + 1) * BLK] = mm3(x, (qh_ref[p, :, cols], ql_ref[p, :, cols]))


def last_rotation(xh, xl, qh, ql):
    rows = xh.shape[0]
    step_rows = rows // 4
    return pl.pallas_call(
        functools.partial(rotate_kernel, step_rows),
        grid=(rows // step_rows,),
        out_shape=jax.ShapeDtypeStruct(xh.shape, f32),
        in_specs=[pl.BlockSpec(memory_space=pltpu.VMEM)] * 4,
        out_specs=pl.BlockSpec((step_rows, 4 * BLK), lambda i: (i, 0)),
        compiler_params=pltpu.CompilerParams(vmem_limit_bytes=20 << 20),
    )(xh, xl, qh, ql)


def shards(n_row, n_col, activations, plan):
    return last_rotation(*two_rounds(plan, activations, n_row, n_col))


def solution(mesh):
    placed = (P("row", "col"), P())
    return jax.shard_map(
        functools.partial(shards, mesh.shape["row"], mesh.shape["col"]),
        mesh=mesh, in_specs=placed, out_specs=P("row", "col"), check_vma=False,
    )
```

```python
import functools
import math

import jax
import jax.numpy as jnp
from jax import lax
from jax.experimental import pallas as pl
from jax.experimental.pallas import tpu as pltpu
from jax.sharding import PartitionSpec as P

BLK = 256
HALF = 128
EPS = 1e-6
STEPS = 7
BOUND = 1.02 * (1.0 + (BLK / 2) ** 2 / 4)
MESH = pl.DeviceIdType.MESH
HIGHEST = lax.Precision.HIGHEST
f32, bf16 = jnp.float32, jnp.bfloat16


def split(value):
    hi = value.astype(bf16)
    return hi, (value - hi.astype(f32)).astype(bf16)


def mm(a, b):
    return lax.dot_general(a, b, (((1,), (0,)), ((), ())), preferred_element_type=f32)


def mm_t(a, b):
    return lax.dot_general(a, b, (((0,), (0,)), ((), ())), preferred_element_type=f32)


def mm3(a, b):
    return mm(a[0], b[0]) + (mm(a[0], b[1]) + mm(a[1], b[0]))


def full(a, b, dims):
    return lax.dot_general(a, b, (dims, ((), ())), precision=HIGHEST, preferred_element_type=f32)


def eye():
    rows = lax.broadcasted_iota(jnp.int32, (BLK, BLK), 0)
    cols = lax.broadcasted_iota(jnp.int32, (BLK, BLK), 1)
    return jnp.where(rows == cols, 1.0, 0.0).astype(f32)


def put_block(i, value, hi_ref, lo_ref, pair, whole_ref=None):
    cells = (((value, 0, 0),), ((value, 0, 1), (-value.T, 1, 0)), ((value, 1, 1),))[i]
    for cell, r, c in cells:
        hi, lo = split(cell)
        hi_ref[pair, r * BLK : (r + 1) * BLK, c * BLK : (c + 1) * BLK] = hi
        lo_ref[pair, r * BLK : (r + 1) * BLK, c * BLK : (c + 1) * BLK] = lo
        if whole_ref is not None:
            whole_ref[2 * pair + c, r] = cell


def rounds_kernel(
    n_row, n_col, rows,
    plan_ref, x_ref, xh_ref, xl_ref, qh_ref, ql_ref,
    xv, nv, zsend, zrecv, gram, sq, part_send, part_recv, rs_src, rs_recv, ag, gmat, cmat, qv, qhi, qlo, qf,
    esend, erecv, zearly, qz, qz_all, qz_other,
    load_sem, part_s, part_r, rs_s, rs_r, ag_s, ag_r, q_s, q_r, z_s, z_r,
    e_s, e_r, qz_s, qz_r, qa_s, qa_r, qp_s, qp_r,
):
    chips = n_row // 2
    crow = BLK // chips
    row, z = lax.axis_index("row"), lax.axis_index("col")
    core, chip = lax.rem(row, 2), row // 2
    other = 1 - core
    partner = (chip * 2 + other, z)
    z_up, z_down = lax.rem(z + 1, n_col), lax.rem(z + n_col - 1, n_col)
    unit = rows // 8
    late = [(0, unit), (unit, 2 * unit), (3 * unit, unit)]
    early, n_early = 4 * unit, 4 * unit

    side = math.isqrt(chips)
    cx, cy = chip // side, lax.rem(chip, side)

    def hops(offset):
        return min(offset, side - offset)

    far_first = sorted(
        [(dx, dy) for dx in range(side) for dy in range(side) if (dx, dy) != (0, 0)],
        key=lambda d: -hops(d[0]) - hops(d[1]),
    )
    peers = []
    for dx, dy in far_first:
        t = lax.rem(cx + dx, side) * side + lax.rem(cy + dy, side)
        peers.append((t, (t * 2 + core, z)))

    loads = []
    for i, p in enumerate((other, core)):
        for h in range(2):
            cols = pl.ds(pl.multiple_of((2 * p + h) * BLK, BLK), BLK)
            loads.append(pltpu.make_async_copy(x_ref.at[:, cols], xv.at[2 * p + h], load_sem.at[2 * i + h]))
            loads[-1].start()

    barrier = pltpu.get_barrier_semaphore()

    for dev in [dev for _, dev in peers] + [(row, z_up), (row, z_down), partner]:
        pl.semaphore_signal(barrier, inc=1, device_id=dev, device_id_type=MESH)

    def gram_step(p, start, step_rows, keep=False):
        rs = pl.ds(start, step_rows)
        lead, mate = xv[2 * p, rs, :], xv[2 * p + 1, rs, :]
        lh, ll = split(lead)
        mh, ml = split(mate)
        if keep:
            for h, hi, lo in ((0, lh, ll), (1, mh, ml)):
                cols = pl.ds(pl.multiple_of((2 * p + h) * BLK, BLK), BLK)
                xh_ref[rs, cols] = hi
                xl_ref[rs, cols] = lo
        gram[p] += mm_t(lh, mh) + (mm_t(lh, ml) + mm_t(ll, mh))
        sq[p, 0] += jnp.sum((lead * lead).reshape(step_rows // 8, 8, BLK), axis=0)
        sq[p, 1] += jnp.sum((mate * mate).reshape(step_rows // 8, 8, BLK), axis=0)

    def squares(p):
        lead_sq = jnp.sum(sq[p, 0], axis=0, keepdims=True)
        mate_sq = jnp.sum(sq[p, 1], axis=0, keepdims=True)
        return jnp.concatenate(
            [lead_sq[:, :HALF], lead_sq[:, HALF:], mate_sq[:, :HALF], mate_sq[:, HALF:], jnp.zeros((4, HALF), f32)],
            axis=0,
        )

    def part_copy(rnd):
        return pltpu.make_async_remote_copy(
            part_send.at[rnd], part_recv.at[rnd], part_s.at[rnd], part_r.at[rnd], device_id=partner, device_id_type=MESH
        )

    def fill_part(rnd):
        part_send[rnd, 0:BLK, :] = gram[other, :, 0:HALF]
        part_send[rnd, BLK : 2 * BLK, :] = gram[other, :, HALF:BLK]
        part_send[rnd, 2 * BLK : 2 * BLK + 8, :] = squares(other)

    def reduce_gram(rnd):
        own_sq = squares(core)
        part_copy(rnd).wait()
        left = gram[core, :, 0:HALF] + part_recv[rnd, 0:BLK, :]
        right = gram[core, :, HALF:BLK] + part_recv[rnd, BLK : 2 * BLK, :]
        both_sq = own_sq + part_recv[rnd, 2 * BLK : 2 * BLK + 8, :]
        rs_src[rnd, :, 0:crow, :] = left.reshape(chips, crow, HALF)
        rs_src[rnd, :, crow : 2 * crow, :] = right.reshape(chips, crow, HALF)
        rs_src[rnd, :, 2 * crow : 2 * crow + 8, :] = jnp.broadcast_to(both_sq[None], (chips, 8, HALF))

        sent = crow * 2 + 4

        def rs_copy(k, t, dev, source):
            return pltpu.make_async_remote_copy(
                rs_src.at[rnd, t, 0:sent], rs_recv.at[rnd, source, 0:sent], rs_s.at[rnd, k], rs_r.at[rnd, source],
                device_id=dev, device_id_type=MESH,
            )

        def ag_copy(k, dev, source):
            return pltpu.make_async_remote_copy(
                ag.at[rnd, source], ag.at[rnd, source], ag_s.at[rnd, k], ag_r.at[rnd, source],
                device_id=dev, device_id_type=MESH,
            )

        for k, (t, dev) in enumerate(peers):
            rs_copy(k, t, dev, chip).start()
        rs_recv[rnd, chip] = rs_src[rnd, chip]
        for k, (t, dev) in enumerate(peers):
            rs_copy(k, t, dev, t).wait_recv()
        total = jnp.sum(rs_recv[rnd], axis=0)
        ag[rnd, chip] = total[0 : 2 * crow]
        for k, (t, dev) in enumerate(peers):
            ag_copy(k, dev, chip).start()
        for k, (t, dev) in enumerate(peers):
            rs_copy(k, t, dev, chip).wait_send()
        for k, (t, dev) in enumerate(peers):
            ag_copy(k, dev, t).wait_recv()
        for k, (t, dev) in enumerate(peers):
            ag_copy(k, dev, chip).wait_send()
        return total[2 * crow : 2 * crow + 8]

    def rotation(rnd, sums, *refs):
        lead_sq = jnp.concatenate([sums[0:1], sums[1:2]], axis=1)
        mate_sq = jnp.concatenate([sums[2:3], sums[3:4]], axis=1)
        lead_col = jnp.broadcast_to(lead_sq, (8, BLK)).T[:, 0:1]
        cross = jnp.concatenate(
            [ag[rnd, :, 0:crow, :].reshape(BLK, HALF), ag[rnd, :, crow : 2 * crow, :].reshape(BLK, HALF)], axis=1
        )
        cmat[...] = cross / (lead_col + mate_sq + EPS)
        ident = eye()
        gmat[...] = ident + 0.25 * full(cmat[...], cmat[...], ((1,), (1,)))
        scale = 2.0 / (1.0 + BOUND)
        radius = (BOUND - 1.0) / (BOUND + 1.0)
        res = split(ident - scale * gmat[...])
        inv = None
        for k in range(STEPS):
            s = 2.0 / (2.0 - radius * radius)
            radius = radius * radius / (2.0 - radius * radius)
            if k < STEPS - 1:
                square = mm3(res, res)
            if k == 0:
                inv = (s * scale) * (ident + (res[0].astype(f32) + res[1].astype(f32)))
            else:
                inv = s * (inv + mm3(split(inv), res))
            if k < STEPS - 1:
                res = split(s * square + (1.0 - s) * ident)
        inv_parts = split(inv)
        inv = inv + mm3(inv_parts, split(ident - mm3(split(gmat[...]), inv_parts)))
        w = full(inv, cmat[...], ((1,), (0,)))
        err = split(ident - full(inv, gmat[...], ((1,), (0,))))
        inv = inv + mm3(err, split(inv))
        send_block(rnd, 0, 2.0 * inv - ident, refs)
        w = w + mm3(err, split(w))
        send_block(rnd, 1, w, refs)
        send_block(rnd, 2, ident - 0.5 * full(cmat[...], w, ((0,), (0,))), refs)

    def send_block(rnd, i, value, refs):
        qv[rnd, core, i] = value
        q_copy(rnd, core, i).start()
        put_block(i, value, refs[0], refs[1], core, *refs[2:])

    def receive_blocks(rnd, *refs):
        for i in range(3):
            q_copy(rnd, other, i).wait_recv()
            put_block(i, qv[rnd, other, i], refs[0], refs[1], other, *refs[2:])
        for i in range(3):
            q_copy(rnd, core, i).wait_send()

    def q_copy(rnd, p, i):
        return pltpu.make_async_remote_copy(
            qv.at[rnd, p, i], qv.at[rnd, p, i], q_s.at[rnd, i], q_r.at[rnd, i], device_id=partner, device_id_type=MESH
        )

    def rotate(p, start, step_rows):
        rs = pl.ds(start, step_rows)
        x = jnp.concatenate([xv[2 * p, rs, :], xv[2 * p + 1, rs, :]], axis=1)
        xh, xl = split(x)
        for h in range(2):
            cols = slice(h * BLK, (h + 1) * BLK)
            nv[2 * p + h, rs, :] = mm3((xh, xl), (qhi[p, :, cols], qlo[p, :, cols]))

    up_slot = down_slot = jnp.int32(0)
    for j in range(4):
        above, below = plan_ref[1, z_up * 4 + j], plan_ref[1, z_down * 4 + j]
        up_slot = jnp.where(above // 4 == z, above - 4 * z, up_slot)
        down_slot = jnp.where(below // 4 == z, below - 4 * z, down_slot)

    def z_copy(way, i):
        rs = pl.ds(*late[i])
        return pltpu.make_async_remote_copy(
            zsend.at[way, rs, :], zrecv.at[way, rs, :], z_s.at[way, i], z_r.at[way, i],
            device_id=(row, z_up if way == 0 else z_down), device_id_type=MESH,
        )

    def early_copy(way):
        return pltpu.make_async_remote_copy(
            esend.at[way], erecv.at[way], e_s.at[way], e_r.at[way],
            device_id=(row, z_up if way == 0 else z_down), device_id_type=MESH,
        )

    def share_copy(way):
        return pltpu.make_async_remote_copy(
            qz.at[way], qz_all.at[chip, way], qz_s.at[way], qz_r.at[way],
            device_id=(row, z_up if way == 0 else z_down), device_id_type=MESH,
        )

    def share_gather(k, dev, source):
        return pltpu.make_async_remote_copy(
            qz_all.at[source], qz_all.at[source], qa_s.at[k], qa_r.at[source], device_id=dev, device_id_type=MESH
        )

    def share_swap():
        return pltpu.make_async_remote_copy(
            qz_all, qz_other, qp_s.at[0], qp_r.at[0], device_id=partner, device_id_type=MESH
        )

    gram[...] = jnp.zeros_like(gram)
    sq[...] = jnp.zeros_like(sq)
    loads[0].wait()
    loads[1].wait()
    for start in range(0, rows, 2 * unit):
        gram_step(other, start, 2 * unit)
    fill_part(0)
    loads[2].wait()
    loads[3].wait()
    for way, slot in enumerate((up_slot, down_slot)):
        for h in range(2):
            esend[way, h] = xv[(slot // 2) * 2 + h, pl.ds(early, n_early), :]
    pl.semaphore_wait(barrier, chips + 2)
    for way in range(2):
        early_copy(way).start()
    part_copy(0).start()
    for start in range(0, rows, 2 * unit):
        gram_step(core, start, 2 * unit)
    rotation(0, reduce_gram(0), qhi, qlo, qf)
    for start, size in late:
        rotate(core, start, size)
    receive_blocks(0, qhi, qlo, qf)
    for way, slot in enumerate((up_slot, down_slot)):
        qz[way] = qf[slot, core, pl.ds(pl.multiple_of(chip * crow, crow), crow), :]
        share_copy(way).start()
    for i, (start, size) in enumerate(late):
        rotate(other, start, size)
        rs = pl.ds(start, size)
        zsend[0, rs, :] = nv[up_slot, rs, :]
        z_copy(0, i).start()
        zsend[1, rs, :] = nv[down_slot, rs, :]
        z_copy(1, i).start()
    for way in range(2):
        share_copy(way).wait_recv()
    for k, (_, dev) in enumerate(peers):
        share_gather(k, dev, chip).start()
    rotate(core, early, n_early)
    rotate(other, early, n_early)

    gram[...] = jnp.zeros_like(gram)
    sq[...] = jnp.zeros_like(sq)

    def place(p, start, size, lower, upper):
        rs = pl.ds(start, size)
        for h in range(2):
            origin = plan_ref[1, z * 4 + 2 * p + h]
            home = origin // 4
            own = nv[jnp.clip(origin - 4 * z, 0, 3), rs, :]
            xv[2 * p + h, rs, :] = jnp.where(home == z, own, jnp.where(home < z, lower[...], upper[...]))
        gram_step(p, start, size, True)

    def arrive(i):
        z_copy(0, i).wait_recv()
        z_copy(1, i).wait_recv()

    def place_late(p, i):
        rs = pl.ds(*late[i])
        place(p, *late[i], zrecv.at[0, rs, :], zrecv.at[1, rs, :])

    arrive(0)
    place_late(other, 0)
    place_late(core, 0)
    for k, (t, dev) in enumerate(peers):
        share_gather(k, dev, t).wait_recv()
    share_swap().start()
    for way in range(2):
        early_copy(way).wait_recv()
    for way in range(2):
        part = qz_all[:, way].reshape(BLK, BLK)
        zearly[way] = mm3(split(erecv[way, core]), split(part))
    arrive(1)
    place_late(other, 1)
    place_late(core, 1)
    share_swap().wait_recv()
    for way in range(2):
        part = qz_other[:, way].reshape(BLK, BLK)
        zearly[way] += mm3(split(erecv[way, other]), split(part))
    place(other, early, n_early, zearly.at[0], zearly.at[1])
    place(core, early, n_early, zearly.at[0], zearly.at[1])
    arrive(2)
    place_late(other, 2)
    fill_part(1)
    part_copy(1).start()
    place_late(core, 2)
    for way in range(2):
        for i in range(len(late)):
            z_copy(way, i).wait_send()
        early_copy(way).wait_send()
        share_copy(way).wait_send()
    for k, (_, dev) in enumerate(peers):
        share_gather(k, dev, chip).wait_send()
    share_swap().wait_send()
    rotation(1, reduce_gram(1), qh_ref, ql_ref)
    receive_blocks(1, qh_ref, ql_ref)


def two_rounds(plan, x, n_row, n_col):
    rows = x.shape[0]
    n_early = rows // 2
    chips = n_row // 2
    crow = BLK // chips
    dma = pltpu.SemaphoreType.DMA
    return pl.pallas_call(
        functools.partial(rounds_kernel, n_row, n_col, rows),
        out_shape=[jax.ShapeDtypeStruct(x.shape, bf16)] * 2 + [jax.ShapeDtypeStruct((2, 2 * BLK, 2 * BLK), bf16)] * 2,
        in_specs=[pl.BlockSpec(memory_space=pltpu.SMEM), pl.BlockSpec(memory_space=pl.ANY)],
        out_specs=[pl.BlockSpec(memory_space=pltpu.VMEM)] * 4,
        scratch_shapes=[
            pltpu.VMEM((4, rows, BLK), f32),
            pltpu.VMEM((4, rows, BLK), f32),
            pltpu.VMEM((2, rows, BLK), f32),
            pltpu.VMEM((2, rows, BLK), f32),
            pltpu.VMEM((2, BLK, BLK), f32),
            pltpu.VMEM((2, 2, 8, BLK), f32),
            pltpu.VMEM((2, 2 * BLK + 8, HALF), f32),
            pltpu.VMEM((2, 2 * BLK + 8, HALF), f32),
            pltpu.VMEM((2, chips, 2 * crow + 8, HALF), f32),
            pltpu.VMEM((2, chips, 2 * crow + 8, HALF), f32),
            pltpu.VMEM((2, chips, 2 * crow, HALF), f32),
            pltpu.VMEM((BLK, BLK), f32),
            pltpu.VMEM((BLK, BLK), f32),
            pltpu.VMEM((2, 2, 3, BLK, BLK), f32),
            pltpu.VMEM((2, 2 * BLK, 2 * BLK), bf16),
            pltpu.VMEM((2, 2 * BLK, 2 * BLK), bf16),
            pltpu.VMEM((4, 2, BLK, BLK), f32),
            pltpu.VMEM((2, 2, n_early, BLK), f32),
            pltpu.VMEM((2, 2, n_early, BLK), f32),
            pltpu.VMEM((2, n_early, BLK), f32),
            pltpu.VMEM((2, crow, BLK), f32),
            pltpu.VMEM((chips, 2, crow, BLK), f32),
            pltpu.VMEM((chips, 2, crow, BLK), f32),
            dma((4,)),
            dma((2,)), dma((2,)),
            dma((2, chips)), dma((2, chips)),
            dma((2, chips)), dma((2, chips)),
            dma((2, 3)), dma((2, 3)),
            dma((2, 3)), dma((2, 3)),
            dma((2,)), dma((2,)),
            dma((2,)), dma((2,)),
            dma((chips,)), dma((chips,)),
            dma((1,)), dma((1,)),
        ],
        compiler_params=pltpu.CompilerParams(collective_id=0, has_side_effects=True, vmem_limit_bytes=46 << 20),
    )(plan, x)


def rotate_kernel(step_rows, xh_ref, xl_ref, qh_ref, ql_ref, o_ref):
    rs = pl.ds(pl.multiple_of(pl.program_id(0) * step_rows, step_rows), step_rows)
    for p in range(2):
        pair = slice(2 * p * BLK, (2 * p + 2) * BLK)
        x = xh_ref[rs, pair], xl_ref[rs, pair]
        for h in range(2):
            cols = slice(h * BLK, (h + 1) * BLK)
            o_ref[:, (2 * p + h) * BLK : (2 * p + h + 1) * BLK] = mm3(x, (qh_ref[p, :, cols], ql_ref[p, :, cols]))


def last_rotation(xh, xl, qh, ql):
    rows = xh.shape[0]
    step_rows = rows // 4
    return pl.pallas_call(
        functools.partial(rotate_kernel, step_rows),
        grid=(rows // step_rows,),
        out_shape=jax.ShapeDtypeStruct(xh.shape, f32),
        in_specs=[pl.BlockSpec(memory_space=pltpu.VMEM)] * 4,
        out_specs=pl.BlockSpec((step_rows, 4 * BLK), lambda i: (i, 0)),
        compiler_params=pltpu.CompilerParams(vmem_limit_bytes=20 << 20),
    )(xh, xl, qh, ql)


def shards(n_row, n_col, activations, plan):
    return last_rotation(*two_rounds(plan, activations, n_row, n_col))


def solution(mesh):
    placed = (P("row", "col"), P())
    return jax.shard_map(
        functools.partial(shards, mesh.shape["row"], mesh.shape["col"]),
        mesh=mesh, in_specs=placed, out_specs=P("row", "col"), check_vma=False,
    )
```

```python
import functools
import math

import jax
import jax.numpy as jnp
from jax import lax
from jax.experimental import pallas as pl
from jax.experimental.pallas import tpu as pltpu
from jax.sharding import PartitionSpec as P

BLK = 256
HALF = 128
EPS = 1e-6
STEPS = 7
BOUND = 1.02 * (1.0 + (BLK / 2) ** 2 / 4)
MESH = pl.DeviceIdType.MESH
HIGHEST = lax.Precision.HIGHEST
f32, bf16 = jnp.float32, jnp.bfloat16


def split(value):
    hi = value.astype(bf16)
    return hi, (value - hi.astype(f32)).astype(bf16)


def mm(a, b):
    return lax.dot_general(a, b, (((1,), (0,)), ((), ())), preferred_element_type=f32)


def mm_t(a, b):
    return lax.dot_general(a, b, (((0,), (0,)), ((), ())), preferred_element_type=f32)


def mm3(a, b):
    return mm(a[0], b[0]) + (mm(a[0], b[1]) + mm(a[1], b[0]))


def full(a, b, dims):
    return lax.dot_general(a, b, (dims, ((), ())), precision=HIGHEST, preferred_element_type=f32)


def eye():
    rows = lax.broadcasted_iota(jnp.int32, (BLK, BLK), 0)
    cols = lax.broadcasted_iota(jnp.int32, (BLK, BLK), 1)
    return jnp.where(rows == cols, 1.0, 0.0).astype(f32)


def put_block(i, value, hi_ref, lo_ref, pair, whole_ref=None):
    cells = (((value, 0, 0),), ((value, 0, 1), (-value.T, 1, 0)), ((value, 1, 1),))[i]
    for cell, r, c in cells:
        hi, lo = split(cell)
        hi_ref[pair, r * BLK : (r + 1) * BLK, c * BLK : (c + 1) * BLK] = hi
        lo_ref[pair, r * BLK : (r + 1) * BLK, c * BLK : (c + 1) * BLK] = lo
        if whole_ref is not None:
            whole_ref[2 * pair + c, r] = cell


def rounds_kernel(
    n_row, n_col, rows,
    plan_ref, x_ref, xh_ref, xl_ref, qh_ref, ql_ref,
    xv, nv, zsend, zrecv, gram, sq, part_send, part_recv, rs_src, rs_recv, ag, gmat, cmat, qv, qhi, qlo, qf,
    esend, erecv, zearly, qz, qz_all, qz_other,
    load_sem, part_s, part_r, rs_s, rs_r, ag_s, ag_r, q_s, q_r, z_s, z_r,
    e_s, e_r, qz_s, qz_r, qa_s, qa_r, qp_s, qp_r,
):
    chips = n_row // 2
    crow = BLK // chips
    row, z = lax.axis_index("row"), lax.axis_index("col")
    core, chip = lax.rem(row, 2), row // 2
    other = 1 - core
    partner = (chip * 2 + other, z)
    z_up, z_down = lax.rem(z + 1, n_col), lax.rem(z + n_col - 1, n_col)
    unit = rows // 8
    late = [(0, 2 * unit), (2 * unit, unit), (3 * unit, unit)]
    early, n_early = 4 * unit, 4 * unit

    side = math.isqrt(chips)
    cx, cy = chip // side, lax.rem(chip, side)

    def hops(offset):
        return min(offset, side - offset)

    far_first = sorted(
        [(dx, dy) for dx in range(side) for dy in range(side) if (dx, dy) != (0, 0)],
        key=lambda d: -hops(d[0]) - hops(d[1]),
    )
    peers = []
    for dx, dy in far_first:
        t = lax.rem(cx + dx, side) * side + lax.rem(cy + dy, side)
        peers.append((t, (t * 2 + core, z)))

    loads = []
    for i, p in enumerate((other, core)):
        for h in range(2):
            cols = pl.ds(pl.multiple_of((2 * p + h) * BLK, BLK), BLK)
            loads.append(pltpu.make_async_copy(x_ref.at[:, cols], xv.at[2 * p + h], load_sem.at[2 * i + h]))
            loads[-1].start()

    barrier = pltpu.get_barrier_semaphore()

    for dev in [dev for _, dev in peers] + [(row, z_up), (row, z_down), partner]:
        pl.semaphore_signal(barrier, inc=1, device_id=dev, device_id_type=MESH)

    def gram_step(p, start, step_rows, keep=False):
        rs = pl.ds(start, step_rows)
        lead, mate = xv[2 * p, rs, :], xv[2 * p + 1, rs, :]
        lh, ll = split(lead)
        mh, ml = split(mate)
        if keep:
            for h, hi, lo in ((0, lh, ll), (1, mh, ml)):
                cols = pl.ds(pl.multiple_of((2 * p + h) * BLK, BLK), BLK)
                xh_ref[rs, cols] = hi
                xl_ref[rs, cols] = lo
        gram[p] += mm_t(lh, mh) + (mm_t(lh, ml) + mm_t(ll, mh))
        sq[p, 0] += jnp.sum((lead * lead).reshape(step_rows // 8, 8, BLK), axis=0)
        sq[p, 1] += jnp.sum((mate * mate).reshape(step_rows // 8, 8, BLK), axis=0)

    def squares(p):
        lead_sq = jnp.sum(sq[p, 0], axis=0, keepdims=True)
        mate_sq = jnp.sum(sq[p, 1], axis=0, keepdims=True)
        return jnp.concatenate(
            [lead_sq[:, :HALF], lead_sq[:, HALF:], mate_sq[:, :HALF], mate_sq[:, HALF:], jnp.zeros((4, HALF), f32)],
            axis=0,
        )

    def part_copy(rnd):
        return pltpu.make_async_remote_copy(
            part_send.at[rnd], part_recv.at[rnd], part_s.at[rnd], part_r.at[rnd], device_id=partner, device_id_type=MESH
        )

    def fill_part(rnd):
        part_send[rnd, 0:BLK, :] = gram[other, :, 0:HALF]
        part_send[rnd, BLK : 2 * BLK, :] = gram[other, :, HALF:BLK]
        part_send[rnd, 2 * BLK : 2 * BLK + 8, :] = squares(other)

    def reduce_gram(rnd):
        own_sq = squares(core)
        part_copy(rnd).wait()
        left = gram[core, :, 0:HALF] + part_recv[rnd, 0:BLK, :]
        right = gram[core, :, HALF:BLK] + part_recv[rnd, BLK : 2 * BLK, :]
        both_sq = own_sq + part_recv[rnd, 2 * BLK : 2 * BLK + 8, :]
        rs_src[rnd, :, 0:crow, :] = left.reshape(chips, crow, HALF)
        rs_src[rnd, :, crow : 2 * crow, :] = right.reshape(chips, crow, HALF)
        rs_src[rnd, :, 2 * crow : 2 * crow + 8, :] = jnp.broadcast_to(both_sq[None], (chips, 8, HALF))

        sent = crow * 2 + 4

        def rs_copy(k, t, dev, source):
            return pltpu.make_async_remote_copy(
                rs_src.at[rnd, t, 0:sent], rs_recv.at[rnd, source, 0:sent], rs_s.at[rnd, k], rs_r.at[rnd, source],
                device_id=dev, device_id_type=MESH,
            )

        def ag_copy(k, dev, source):
            return pltpu.make_async_remote_copy(
                ag.at[rnd, source], ag.at[rnd, source], ag_s.at[rnd, k], ag_r.at[rnd, source],
                device_id=dev, device_id_type=MESH,
            )

        for k, (t, dev) in enumerate(peers):
            rs_copy(k, t, dev, chip).start()
        rs_recv[rnd, chip] = rs_src[rnd, chip]
        for k, (t, dev) in enumerate(peers):
            rs_copy(k, t, dev, t).wait_recv()
        total = jnp.sum(rs_recv[rnd], axis=0)
        ag[rnd, chip] = total[0 : 2 * crow]
        for k, (t, dev) in enumerate(peers):
            ag_copy(k, dev, chip).start()
        for k, (t, dev) in enumerate(peers):
            rs_copy(k, t, dev, chip).wait_send()
        for k, (t, dev) in enumerate(peers):
            ag_copy(k, dev, t).wait_recv()
        for k, (t, dev) in enumerate(peers):
            ag_copy(k, dev, chip).wait_send()
        return total[2 * crow : 2 * crow + 8]

    def rotation(rnd, sums, *refs):
        lead_sq = jnp.concatenate([sums[0:1], sums[1:2]], axis=1)
        mate_sq = jnp.concatenate([sums[2:3], sums[3:4]], axis=1)
        lead_col = jnp.broadcast_to(lead_sq, (8, BLK)).T[:, 0:1]
        cross = jnp.concatenate(
            [ag[rnd, :, 0:crow, :].reshape(BLK, HALF), ag[rnd, :, crow : 2 * crow, :].reshape(BLK, HALF)], axis=1
        )
        cmat[...] = cross / (lead_col + mate_sq + EPS)
        ident = eye()
        gmat[...] = ident + 0.25 * full(cmat[...], cmat[...], ((1,), (1,)))
        scale = 2.0 / (1.0 + BOUND)
        radius = (BOUND - 1.0) / (BOUND + 1.0)
        res = split(ident - scale * gmat[...])
        inv = None
        for k in range(STEPS):
            s = 2.0 / (2.0 - radius * radius)
            radius = radius * radius / (2.0 - radius * radius)
            if k < STEPS - 1:
                square = mm3(res, res)
            if k == 0:
                inv = (s * scale) * (ident + (res[0].astype(f32) + res[1].astype(f32)))
            else:
                inv = s * (inv + mm3(split(inv), res))
            if k < STEPS - 1:
                res = split(s * square + (1.0 - s) * ident)
        inv_parts = split(inv)
        inv = inv + mm3(inv_parts, split(ident - mm3(split(gmat[...]), inv_parts)))
        w = full(inv, cmat[...], ((1,), (0,)))
        err = split(ident - full(inv, gmat[...], ((1,), (0,))))
        inv = inv + mm3(err, split(inv))
        send_block(rnd, 0, 2.0 * inv - ident, refs)
        w = w + mm3(err, split(w))
        send_block(rnd, 1, w, refs)
        send_block(rnd, 2, ident - 0.5 * full(cmat[...], w, ((0,), (0,))), refs)

    def send_block(rnd, i, value, refs):
        qv[rnd, core, i] = value
        q_copy(rnd, core, i).start()
        put_block(i, value, refs[0], refs[1], core, *refs[2:])

    def receive_blocks(rnd, *refs):
        for i in range(3):
            q_copy(rnd, other, i).wait_recv()
            put_block(i, qv[rnd, other, i], refs[0], refs[1], other, *refs[2:])
        for i in range(3):
            q_copy(rnd, core, i).wait_send()

    def q_copy(rnd, p, i):
        return pltpu.make_async_remote_copy(
            qv.at[rnd, p, i], qv.at[rnd, p, i], q_s.at[rnd, i], q_r.at[rnd, i], device_id=partner, device_id_type=MESH
        )

    def rotate(p, start, step_rows):
        rs = pl.ds(start, step_rows)
        x = jnp.concatenate([xv[2 * p, rs, :], xv[2 * p + 1, rs, :]], axis=1)
        xh, xl = split(x)
        for h in range(2):
            cols = slice(h * BLK, (h + 1) * BLK)
            nv[2 * p + h, rs, :] = mm3((xh, xl), (qhi[p, :, cols], qlo[p, :, cols]))

    up_slot = down_slot = jnp.int32(0)
    for j in range(4):
        above, below = plan_ref[1, z_up * 4 + j], plan_ref[1, z_down * 4 + j]
        up_slot = jnp.where(above // 4 == z, above - 4 * z, up_slot)
        down_slot = jnp.where(below // 4 == z, below - 4 * z, down_slot)

    def z_copy(way, i):
        rs = pl.ds(*late[i])
        return pltpu.make_async_remote_copy(
            zsend.at[way, rs, :], zrecv.at[way, rs, :], z_s.at[way, i], z_r.at[way, i],
            device_id=(row, z_up if way == 0 else z_down), device_id_type=MESH,
        )

    def early_copy(way):
        return pltpu.make_async_remote_copy(
            esend.at[way], erecv.at[way], e_s.at[way], e_r.at[way],
            device_id=(row, z_up if way == 0 else z_down), device_id_type=MESH,
        )

    def share_copy(way):
        return pltpu.make_async_remote_copy(
            qz.at[way], qz_all.at[chip, way], qz_s.at[way], qz_r.at[way],
            device_id=(row, z_up if way == 0 else z_down), device_id_type=MESH,
        )

    def share_gather(k, dev, source):
        return pltpu.make_async_remote_copy(
            qz_all.at[source], qz_all.at[source], qa_s.at[k], qa_r.at[source], device_id=dev, device_id_type=MESH
        )

    def share_swap():
        return pltpu.make_async_remote_copy(
            qz_all, qz_other, qp_s.at[0], qp_r.at[0], device_id=partner, device_id_type=MESH
        )

    gram[...] = jnp.zeros_like(gram)
    sq[...] = jnp.zeros_like(sq)
    loads[0].wait()
    loads[1].wait()
    for start in range(0, rows, 2 * unit):
        gram_step(other, start, 2 * unit)
    fill_part(0)
    loads[2].wait()
    loads[3].wait()
    for way, slot in enumerate((up_slot, down_slot)):
        for h in range(2):
            esend[way, h] = xv[(slot // 2) * 2 + h, pl.ds(early, n_early), :]
    pl.semaphore_wait(barrier, chips + 2)
    for way in range(2):
        early_copy(way).start()
    part_copy(0).start()
    for start in range(0, rows, 2 * unit):
        gram_step(core, start, 2 * unit)
    rotation(0, reduce_gram(0), qhi, qlo, qf)
    for start, size in late:
        rotate(core, start, size)
    receive_blocks(0, qhi, qlo, qf)
    for way, slot in enumerate((up_slot, down_slot)):
        qz[way] = qf[slot, core, pl.ds(pl.multiple_of(chip * crow, crow), crow), :]
        share_copy(way).start()
    for i, (start, size) in enumerate(late):
        rotate(other, start, size)
        rs = pl.ds(start, size)
        zsend[0, rs, :] = nv[up_slot, rs, :]
        z_copy(0, i).start()
        zsend[1, rs, :] = nv[down_slot, rs, :]
        z_copy(1, i).start()
    for way in range(2):
        share_copy(way).wait_recv()
    for k, (_, dev) in enumerate(peers):
        share_gather(k, dev, chip).start()
    rotate(core, early, n_early)
    rotate(other, early, n_early)

    gram[...] = jnp.zeros_like(gram)
    sq[...] = jnp.zeros_like(sq)

    def place(p, start, size, lower, upper):
        rs = pl.ds(start, size)
        for h in range(2):
            origin = plan_ref[1, z * 4 + 2 * p + h]
            home = origin // 4
            own = nv[jnp.clip(origin - 4 * z, 0, 3), rs, :]
            xv[2 * p + h, rs, :] = jnp.where(home == z, own, jnp.where(home < z, lower[...], upper[...]))
        gram_step(p, start, size, True)

    def arrive(i):
        z_copy(0, i).wait_recv()
        z_copy(1, i).wait_recv()

    def place_late(p, i):
        rs = pl.ds(*late[i])
        place(p, *late[i], zrecv.at[0, rs, :], zrecv.at[1, rs, :])

    arrive(0)
    place_late(other, 0)
    place_late(core, 0)
    for k, (t, dev) in enumerate(peers):
        share_gather(k, dev, t).wait_recv()
    share_swap().start()
    for way in range(2):
        early_copy(way).wait_recv()
    for way in range(2):
        part = qz_all[:, way].reshape(BLK, BLK)
        zearly[way] = mm3(split(erecv[way, core]), split(part))
    arrive(1)
    place_late(other, 1)
    place_late(core, 1)
    share_swap().wait_recv()
    for way in range(2):
        part = qz_other[:, way].reshape(BLK, BLK)
        zearly[way] += mm3(split(erecv[way, other]), split(part))
    place(other, early, n_early, zearly.at[0], zearly.at[1])
    place(core, early, n_early, zearly.at[0], zearly.at[1])
    arrive(2)
    place_late(other, 2)
    fill_part(1)
    part_copy(1).start()
    place_late(core, 2)
    rotation(1, reduce_gram(1), qh_ref, ql_ref)
    for way in range(2):
        for i in range(len(late)):
            z_copy(way, i).wait_send()
        early_copy(way).wait_send()
        share_copy(way).wait_send()
    for k, (_, dev) in enumerate(peers):
        share_gather(k, dev, chip).wait_send()
    share_swap().wait_send()
    receive_blocks(1, qh_ref, ql_ref)


def two_rounds(plan, x, n_row, n_col):
    rows = x.shape[0]
    n_early = rows // 2
    chips = n_row // 2
    crow = BLK // chips
    dma = pltpu.SemaphoreType.DMA
    return pl.pallas_call(
        functools.partial(rounds_kernel, n_row, n_col, rows),
        out_shape=[jax.ShapeDtypeStruct(x.shape, bf16)] * 2 + [jax.ShapeDtypeStruct((2, 2 * BLK, 2 * BLK), bf16)] * 2,
        in_specs=[pl.BlockSpec(memory_space=pltpu.SMEM), pl.BlockSpec(memory_space=pl.ANY)],
        out_specs=[pl.BlockSpec(memory_space=pltpu.VMEM)] * 4,
        scratch_shapes=[
            pltpu.VMEM((4, rows, BLK), f32),
            pltpu.VMEM((4, rows, BLK), f32),
            pltpu.VMEM((2, rows, BLK), f32),
            pltpu.VMEM((2, rows, BLK), f32),
            pltpu.VMEM((2, BLK, BLK), f32),
            pltpu.VMEM((2, 2, 8, BLK), f32),
            pltpu.VMEM((2, 2 * BLK + 8, HALF), f32),
            pltpu.VMEM((2, 2 * BLK + 8, HALF), f32),
            pltpu.VMEM((2, chips, 2 * crow + 8, HALF), f32),
            pltpu.VMEM((2, chips, 2 * crow + 8, HALF), f32),
            pltpu.VMEM((2, chips, 2 * crow, HALF), f32),
            pltpu.VMEM((BLK, BLK), f32),
            pltpu.VMEM((BLK, BLK), f32),
            pltpu.VMEM((2, 2, 3, BLK, BLK), f32),
            pltpu.VMEM((2, 2 * BLK, 2 * BLK), bf16),
            pltpu.VMEM((2, 2 * BLK, 2 * BLK), bf16),
            pltpu.VMEM((4, 2, BLK, BLK), f32),
            pltpu.VMEM((2, 2, n_early, BLK), f32),
            pltpu.VMEM((2, 2, n_early, BLK), f32),
            pltpu.VMEM((2, n_early, BLK), f32),
            pltpu.VMEM((2, crow, BLK), f32),
            pltpu.VMEM((chips, 2, crow, BLK), f32),
            pltpu.VMEM((chips, 2, crow, BLK), f32),
            dma((4,)),
            dma((2,)), dma((2,)),
            dma((2, chips)), dma((2, chips)),
            dma((2, chips)), dma((2, chips)),
            dma((2, 3)), dma((2, 3)),
            dma((2, 3)), dma((2, 3)),
            dma((2,)), dma((2,)),
            dma((2,)), dma((2,)),
            dma((chips,)), dma((chips,)),
            dma((1,)), dma((1,)),
        ],
        compiler_params=pltpu.CompilerParams(collective_id=0, has_side_effects=True, vmem_limit_bytes=46 << 20),
    )(plan, x)


def rotate_kernel(step_rows, xh_ref, xl_ref, qh_ref, ql_ref, o_ref):
    rs = pl.ds(pl.multiple_of(pl.program_id(0) * step_rows, step_rows), step_rows)
    for p in range(2):
        pair = slice(2 * p * BLK, (2 * p + 2) * BLK)
        x = xh_ref[rs, pair], xl_ref[rs, pair]
        for h in range(2):
            cols = slice(h * BLK, (h + 1) * BLK)
            o_ref[:, (2 * p + h) * BLK : (2 * p + h + 1) * BLK] = mm3(x, (qh_ref[p, :, cols], ql_ref[p, :, cols]))


def last_rotation(xh, xl, qh, ql):
    rows = xh.shape[0]
    step_rows = rows // 4
    return pl.pallas_call(
        functools.partial(rotate_kernel, step_rows),
        grid=(rows // step_rows,),
        out_shape=jax.ShapeDtypeStruct(xh.shape, f32),
        in_specs=[pl.BlockSpec(memory_space=pltpu.VMEM)] * 4,
        out_specs=pl.BlockSpec((step_rows, 4 * BLK), lambda i: (i, 0)),
        compiler_params=pltpu.CompilerParams(vmem_limit_bytes=20 << 20),
    )(xh, xl, qh, ql)


def shards(n_row, n_col, activations, plan):
    return last_rotation(*two_rounds(plan, activations, n_row, n_col))


def solution(mesh):
    placed = (P("row", "col"), P())
    return jax.shard_map(
        functools.partial(shards, mesh.shape["row"], mesh.shape["col"]),
        mesh=mesh, in_specs=placed, out_specs=P("row", "col"), check_vma=False,
    )
```
